512 devices in a mesh: dom: 16 (over z_lo, x, core), band: 32 (over z_hi, y).
Axes of the slice: x: 4, y: 8, z: 8 (z_hi: 4, z_lo: 2; z = z_hi * 2 + z_lo), core: 2. Of those that a mesh axis runs over, the one named last changes fastest.
Arguments:
- orbitals: bfloat16 [1024, 16, 2, 16, 128], P('band', 'dom'), may hold values from -6 to 6
- potential: float32 [16, 2, 16, 128], P('dom'), may hold values from -1 to 1
- ritz: bfloat16 [1024, 1024], P(None, 'band'), may hold values from -0.1875 to 0.1875
Outputs:
- rotated: float32 [1024, 16, 2, 16, 128], P('band', 'dom')
The draws below stay inside these ranges and needn't reach their ends.
All inputs are finite; a program needn't handle non-finite values.
Results may differ from the reference program's by a relative error of at most 0.0029.
Values may be sent and summed in bfloat16 or wider, within the bound.
No kernel may reach another device: no remote copies, remote signals or barrier semaphores. Data moves between devices by JAX's collectives and lax.ppermute only.
A program may use at most 64 MiB of HBM per device.

```python
import math
import jax
import jax.numpy as jnp
from jax import lax

NB = 1024
CX = 2
CY = 16
NZ = 128
DEG = 4
N_DOM = 16


def level_of(rng, shape, shards, least, top_value):
    def one(position, blocks):
        steps = jax.random.uniform(jax.random.fold_in(jax.random.fold_in(rng, 6), position), (blocks,), jnp.float32, least / len(shards), top_value / len(shards))
        return jnp.repeat(jnp.exp(steps), shape[position] // blocks).reshape((-1,) + (1,) * (len(shape) - position - 1))

    factor_of = one(*shards[0])
    for cut in shards[1:]:
        factor_of = factor_of * one(*cut)
    return factor_of


def normal_values(stream_key, shape, deviation, bound, pieces=(), kind=jnp.bfloat16):
    drawn = deviation * jax.random.normal(stream_key, shape, jnp.float32)
    if pieces:
        drawn = drawn * level_of(stream_key, shape, pieces, -0.22, 0.18)
    return jnp.clip(drawn, -bound, bound).astype(kind)


def setup_inputs(seed: int = 0) -> dict:
    splits = jax.random.split(jax.random.key(seed), 4)
    orbitals = normal_values(splits[0], (NB, N_DOM, CX, CY, NZ), 1.0, 6.0, ((0, 32), (1, 16)))
    potential = jnp.clip(jax.random.uniform(splits[1], (N_DOM, CX, CY, NZ), jnp.float32, -1.0, 1.0) * level_of(splits[1], (N_DOM, CX, CY, NZ), ((0, 16),), -0.4, 0.0), -1.0, 1.0)
    ritz = normal_values(splits[2], (NB, NB), NB ** -0.5, 0.1875, ((1, 32),))
    return dict(orbitals=orbitals, potential=potential, ritz=ritz)


lower_bound = -1.5
cut_off = 1.0
upper_bound = 9.5
coef_zero = -2.5
coef_one = 4.0 / 3.0
coef_two = -1.0 / 12.0

def filter_weights(degree):
    half_width = (upper_bound - cut_off) / 2.0
    centre = (upper_bound + cut_off) / 2.0
    sigma_now = half_width / (lower_bound - centre)
    first_scale = sigma_now / half_width
    inverse_gain = 2.0 / sigma_now
    weights = []
    for degree_step in range(1, degree):
        sigma_next = 1.0 / (inverse_gain - sigma_now)
        weights.append((2.0 * sigma_next / half_width, sigma_now * sigma_next))
        sigma_now = sigma_next
    return (centre, first_scale, weights)

def second_along(grid, axis):
    near_sum = jnp.roll(grid, 1, axis) + jnp.roll(grid, -1, axis)
    far_sum = jnp.roll(grid, 2, axis) + jnp.roll(grid, -2, axis)
    return coef_one * near_sum + coef_two * far_sum

def hamiltonian(grid, grid_pot):
    second = 3.0 * coef_zero * grid + second_along(grid, 1) + second_along(grid, 2) + second_along(grid, 3)
    return -0.5 * second + grid_pot * grid

def reference(orbitals, potential, ritz):
    grid_side = math.isqrt(N_DOM)
    block_size = math.gcd(NB, 64)
    centre, first_scale, weights = filter_weights(DEG)
    grid_pot = potential.reshape(grid_side, grid_side, CX, CY, NZ).transpose(0, 2, 1, 3, 4)
    grid_pot = grid_pot.reshape(grid_side * CX, grid_side * CY, NZ)
    grid_orb = orbitals.reshape(NB, grid_side, grid_side, CX, CY, NZ).transpose(0, 1, 3, 2, 4, 5)
    grid_orb = grid_orb.reshape(NB // block_size, block_size, grid_side * CX, grid_side * CY, NZ)

    def filter_block(start_block):
        previous = start_block.astype(jnp.float32)
        current = (hamiltonian(previous, grid_pot) - centre * previous) * first_scale
        for scale_h, scale_x in weights:
            following = (hamiltonian(current, grid_pot) - centre * current) * scale_h - scale_x * previous
            previous, current = (current, following)
        return current.astype(jnp.bfloat16)
    filtered = lax.map(filter_block, grid_orb)
    rotated = jnp.dot(ritz.T, filtered.reshape(NB, -1), preferred_element_type=jnp.float32)
    rotated = rotated.reshape(NB, grid_side, CX, grid_side, CY, NZ).transpose(0, 1, 3, 2, 4, 5)
    return rotated.reshape(NB, N_DOM, CX, CY, NZ)
```

```python
import math

import jax
import jax.numpy as jnp
from jax import lax
from jax.experimental import pallas as pl
from jax.experimental.pallas import tpu as pltpu
from jax.sharding import PartitionSpec as P

DEG = 4

lower_bound = -1.5
cut_off = 1.0
upper_bound = 9.5
coef_zero = -2.5
coef_one = 4.0 / 3.0
coef_two = -1.0 / 12.0

PAD = 8


def filter_weights(degree):
    half_width = (upper_bound - cut_off) / 2.0
    centre = (upper_bound + cut_off) / 2.0
    sigma_now = half_width / (lower_bound - centre)
    first_scale = sigma_now / half_width
    inverse_gain = 2.0 / sigma_now
    weights = []
    for degree_step in range(1, degree):
        sigma_next = 1.0 / (inverse_gain - sigma_now)
        weights.append((2.0 * sigma_next / half_width, sigma_now * sigma_next))
        sigma_now = sigma_next
    return (centre, first_scale, weights)


def filter_kernel(n_dom, n_own, cx, cy, nz):
    side = math.isqrt(n_dom)
    gx, gy = side * cx, side * cy
    centre, first_scale, weights = filter_weights(DEG)
    row_stride = n_dom * n_own
    far_near = coef_two / coef_one

    def wrap(ref, band, x):
        ref[band, x, 0:PAD, :] = ref[band, x, gy : gy + PAD, :]
        ref[band, x, PAD + gy : PAD + gy + PAD, :] = ref[band, x, PAD : 2 * PAD, :]

    def shifted_ham(cur, diag, band, x):
        mid = cur[band, x, PAD : PAD + gy, :]

        def plane(step):
            return cur[band, lax.rem(x + (gx + step), gx), PAD : PAD + gy, :]

        def rows(step):
            return cur[band, x, PAD + step : PAD + step + gy, :]

        def lanes(step):
            return pltpu.roll(mid, step % nz, 1)

        near = (plane(-1) + plane(1)) + (rows(-1) + rows(1)) + (lanes(-1) + lanes(1))
        far = (plane(-2) + plane(2)) + (rows(-2) + rows(2)) + (lanes(-2) + lanes(2))
        return diag[x] * mid + (-0.5 * coef_one) * (near + far_near * far)

    def body(blocks, out, first, second, diag, ordered):
        def load(x, carry):
            for j in range(side):
                dom = lax.div(x, cx) * side + j
                inner = lax.rem(x, cx)
                for band in range(n_own):
                    first[band, x, PAD + j * cy : PAD + (j + 1) * cy, :] = blocks[
                        dom, band, inner
                    ].astype(jnp.float32)
                pot = blocks[dom, n_own, inner].astype(jnp.float32) + blocks[
                    dom, n_own + 1, inner
                ].astype(jnp.float32)
                diag[x, j * cy : (j + 1) * cy, :] = pot + (-1.5 * coef_zero - centre)
            for band in range(n_own):
                wrap(first, band, x)
            return carry

        lax.fori_loop(0, gx, load, 0)

        def run(step):
            def one(n, carry):
                step(lax.div(n, gx), lax.rem(n, gx))
                return carry

            lax.fori_loop(0, n_own * gx, one, 0)

        def start(band, x):
            second[band, x, PAD : PAD + gy, :] = shifted_ham(first, diag, band, x) * first_scale
            wrap(second, band, x)

        run(start)
        previous, current = first, second
        for scale_h, scale_x in weights[:-1]:

            def middle(band, x, previous=previous, current=current, scale_h=scale_h, scale_x=scale_x):
                following = shifted_ham(current, diag, band, x) * scale_h
                following = following - scale_x * previous[band, x, PAD : PAD + gy, :]
                previous[band, x, PAD : PAD + gy, :] = following
                wrap(previous, band, x)

            run(middle)
            previous, current = current, previous
        scale_h, scale_x = weights[-1]

        def last(band, x):
            following = shifted_ham(current, diag, band, x) * scale_h
            following = following - scale_x * previous[band, x, PAD : PAD + gy, :]
            for j in range(side):
                for part in range(cy // 8):
                    dom = lax.div(x, cx) * side + j
                    cell = lax.rem(x, cx) * cy + part * 8
                    base = cell * row_stride + dom * n_own + band
                    at = j * cy + part * 8
                    ordered[pl.ds(base, 8, stride=row_stride), :] = following[at : at + 8]

        run(last)
        block = 64

        def store(n, carry):
            at = pl.multiple_of(n * block, block)
            out[pl.ds(at, block), :] = ordered[pl.ds(at, block), :].astype(jnp.bfloat16)
            return carry

        lax.fori_loop(0, out.shape[0] // block, store, 0)

    padded = pltpu.VMEM((n_own, gx, gy + 2 * PAD, nz), jnp.float32)
    rows_out = cx * cy * n_dom * n_own
    return pl.pallas_call(
        body,
        out_shape=jax.ShapeDtypeStruct((rows_out, nz), jnp.bfloat16),
        in_specs=[pl.BlockSpec(memory_space=pltpu.VMEM)],
        out_specs=pl.BlockSpec(memory_space=pltpu.VMEM),
        scratch_shapes=[
            padded,
            padded,
            pltpu.VMEM((gx, gy, nz), jnp.float32),
            pltpu.VMEM((rows_out, nz), jnp.float32),
        ],
        name="chebyshev",
    )


def on_device(orbitals, potential, ritz):
    n_dom = lax.axis_size("dom")
    n_band = lax.axis_size("band")
    n_mine, _, cx, cy, nz = orbitals.shape
    n_all = ritz.shape[0]
    n_own = n_mine // n_dom
    half = n_all // 2
    core = lax.rem(lax.axis_index("dom"), 2)

    columns = ritz.T
    piece = lax.dynamic_slice_in_dim(columns, core * half, half, 1)
    many = jnp.broadcast_to(piece[None], (n_band,) + piece.shape)
    with jax.named_scope("ritz"):
        mine = lax.all_to_all(many, "band", 0, 0, tiled=True).reshape(n_all, half)
        other = lax.ppermute(mine, "dom", [(d, d ^ 1) for d in range(n_dom)])

    pot = potential[0]
    high = lax.reduce_precision(pot, 8, 7)
    parts = jnp.stack([high, pot - high]).astype(jnp.bfloat16)
    parts = jnp.broadcast_to(parts[None], (n_dom, 2, cx, cy, nz))
    blocks = orbitals.reshape(n_dom, n_own, cx, cy, nz)
    blocks = jnp.concatenate([blocks, parts], axis=1)
    with jax.named_scope("spread"):
        blocks = lax.all_to_all(blocks, "dom", 0, 0, tiled=True)
    filtered = filter_kernel(n_dom, n_own, cx, cy, nz)(blocks)

    with jax.named_scope("turn"):
        rows = lax.all_to_all(
            filtered.reshape(n_band * n_dom, n_own, nz), ("band", "dom"), 0, 0, tiled=True
        ).reshape(n_all, nz)

    def product(left, which):
        right = lax.dynamic_slice_in_dim(rows, which * half, half, 0)
        return jnp.dot(left, right, preferred_element_type=jnp.float32)

    rotated = product(mine, core) + product(other, 1 - core)
    rotated = rotated.astype(jnp.bfloat16).reshape(n_band, n_mine, nz)
    with jax.named_scope("back"):
        rotated = lax.all_to_all(rotated, "band", 0, 0, tiled=True)
    rotated = rotated.transpose(1, 0, 2).astype(jnp.float32)
    return rotated.reshape(orbitals.shape)


def solution(mesh):
    in_specs = (P("band", "dom", None, None, None), P("dom", None, None, None), P(None, "band"))
    out_specs = P("band", "dom", None, None, None)
    return jax.shard_map(
        on_device, mesh=mesh, in_specs=in_specs, out_specs=out_specs, check_vma=False
    )
```

```python
import math

import jax
import jax.numpy as jnp
from jax import lax
from jax.experimental import pallas as pl
from jax.experimental.pallas import tpu as pltpu
from jax.sharding import PartitionSpec as P


DEG = 4

lower_bound = -1.5
cut_off = 1.0
upper_bound = 9.5
coef_zero = -2.5
coef_one = 4.0 / 3.0
coef_two = -1.0 / 12.0

PAD = 8


def filter_weights(degree):
    half_width = (upper_bound - cut_off) / 2.0
    centre = (upper_bound + cut_off) / 2.0
    sigma_now = half_width / (lower_bound - centre)
    first_scale = sigma_now / half_width
    inverse_gain = 2.0 / sigma_now
    weights = []
    for _ in range(1, degree):
        sigma_next = 1.0 / (inverse_gain - sigma_now)
        weights.append((2.0 * sigma_next / half_width, sigma_now * sigma_next))
        sigma_now = sigma_next
    return (centre, first_scale, weights)


def filter_kernel(n_dom, n_own, cx, cy, nz):
    side = math.isqrt(n_dom)
    gx, gy = side * cx, side * cy
    centre, first_scale, weights = filter_weights(DEG)
    row_stride = n_dom * n_own
    far_near = coef_two / coef_one

    def wrap(ref, band, x):
        ref[band, x, 0:PAD, :] = ref[band, x, gy : gy + PAD, :]
        ref[band, x, PAD + gy : PAD + gy + PAD, :] = ref[band, x, PAD : 2 * PAD, :]

    def shifted_ham(cur, diag, band, x):
        mid = cur[band, x, PAD : PAD + gy, :]

        def plane(step):
            return cur[band, lax.rem(x + (gx + step), gx), PAD : PAD + gy, :]

        def rows(step):
            return cur[band, x, PAD + step : PAD + step + gy, :]

        def lanes(step):
            return pltpu.roll(mid, step % nz, 1)

        near = (plane(-1) + plane(1)) + (rows(-1) + rows(1)) + (lanes(-1) + lanes(1))
        far = (plane(-2) + plane(2)) + (rows(-2) + rows(2)) + (lanes(-2) + lanes(2))
        return diag[x] * mid + (-0.5 * coef_one) * (near + far_near * far)

    def body(blocks, out, first, second, diag, ordered):
        def load(x, carry):
            for j in range(side):
                dom = lax.div(x, cx) * side + j
                inner = lax.rem(x, cx)
                for band in range(n_own):
                    first[band, x, PAD + j * cy : PAD + (j + 1) * cy, :] = blocks[
                        dom, band, inner
                    ].astype(jnp.float32)
                pot = blocks[dom, n_own, inner].astype(jnp.float32) + blocks[
                    dom, n_own + 1, inner
                ].astype(jnp.float32)
                diag[x, j * cy : (j + 1) * cy, :] = pot + (-1.5 * coef_zero - centre)
            for band in range(n_own):
                wrap(first, band, x)
            return carry

        lax.fori_loop(0, gx, load, 0)

        def run(step):
            def one(n, carry):
                step(lax.div(n, gx), lax.rem(n, gx))
                return carry

            lax.fori_loop(0, n_own * gx, one, 0)

        def start(band, x):
            second[band, x, PAD : PAD + gy, :] = shifted_ham(first, diag, band, x) * first_scale
            wrap(second, band, x)

        run(start)
        previous, current = first, second
        for scale_h, scale_x in weights[:-1]:

            def middle(band, x, previous=previous, current=current, scale_h=scale_h, scale_x=scale_x):
                following = shifted_ham(current, diag, band, x) * scale_h
                following = following - scale_x * previous[band, x, PAD : PAD + gy, :]
                previous[band, x, PAD : PAD + gy, :] = following
                wrap(previous, band, x)

            run(middle)
            previous, current = current, previous
        scale_h, scale_x = weights[-1]

        def last(band, x):
            following = shifted_ham(current, diag, band, x) * scale_h
            following = following - scale_x * previous[band, x, PAD : PAD + gy, :]
            for j in range(side):
                for part in range(cy // 8):
                    dom = lax.div(x, cx) * side + j
                    cell = lax.rem(x, cx) * cy + part * 8
                    base = cell * row_stride + dom * n_own + band
                    at = j * cy + part * 8
                    ordered[pl.ds(base, 8, stride=row_stride), :] = following[at : at + 8]

        run(last)
        block = 64

        def store(n, carry):
            at = pl.multiple_of(n * block, block)
            out[pl.ds(at, block), :] = ordered[pl.ds(at, block), :].astype(jnp.bfloat16)
            return carry

        lax.fori_loop(0, out.shape[0] // block, store, 0)

    padded = pltpu.VMEM((n_own, gx, gy + 2 * PAD, nz), jnp.float32)
    rows_out = cx * cy * n_dom * n_own
    return pl.pallas_call(
        body,
        out_shape=jax.ShapeDtypeStruct((rows_out, nz), jnp.bfloat16),
        in_specs=[pl.BlockSpec(memory_space=pltpu.VMEM)],
        out_specs=pl.BlockSpec(memory_space=pltpu.VMEM),
        scratch_shapes=[
            padded,
            padded,
            pltpu.VMEM((gx, gy, nz), jnp.float32),
            pltpu.VMEM((rows_out, nz), jnp.float32),
        ],
        name="chebyshev",
    )


def rotate_kernel(n_band, order, n_mine, half, nz):
    n_all = n_band * n_mine

    def body(place, mine, other, rows, out, sums):
        core = place[1]
        near = rows[pl.ds(pl.multiple_of(core * half, half), half), :]
        far = rows[pl.ds(pl.multiple_of((1 - core) * half, half), half), :]
        sums[...] = jnp.dot(
            mine[...], near, preferred_element_type=jnp.float32
        ) + jnp.dot(other[...], far, preferred_element_type=jnp.float32)
        for r, mask in enumerate(order):
            at = pl.multiple_of(lax.bitwise_xor(place[0], mask) * n_mine, n_mine)
            out[pl.ds(at, n_mine), :] = sums[r * n_mine : (r + 1) * n_mine, :].astype(jnp.bfloat16)

    vmem = pl.BlockSpec(memory_space=pltpu.VMEM)
    return pl.pallas_call(
        body,
        out_shape=jax.ShapeDtypeStruct((n_all, nz), jnp.bfloat16),
        in_specs=[pl.BlockSpec(memory_space=pltpu.SMEM), vmem, vmem, vmem],
        out_specs=vmem,
        scratch_shapes=[pltpu.VMEM((n_all, nz), jnp.float32)],
        name="rotate",
    )


def in_vmem(x):
    return pltpu.with_memory_space_constraint(x, pltpu.VMEM)


def on_device(orbitals, potential, ritz):
    n_dom = lax.axis_size("dom")
    n_band = lax.axis_size("band")
    n_mine, _, cx, cy, nz = orbitals.shape
    n_all = ritz.shape[0]
    n_own = n_mine // n_dom
    half = n_all // 2
    core = lax.rem(lax.axis_index("dom"), 2)
    band = lax.axis_index("band")

    pot = potential[0]
    high = lax.reduce_precision(pot, 8, 7)
    parts = jnp.stack([high, pot - high]).astype(jnp.bfloat16)
    parts = jnp.broadcast_to(parts[None], (n_dom, 2, cx, cy, nz))
    blocks = orbitals.reshape(n_dom, n_own, cx, cy, nz)
    blocks = jnp.concatenate([blocks, parts], axis=1)
    blocks = lax.all_to_all(blocks, "dom", 0, 0, tiled=True)
    filtered = filter_kernel(n_dom, n_own, cx, cy, nz)(in_vmem(blocks))

    mine = lax.dynamic_slice_in_dim(ritz.T, core * half, half, 1)
    order = [0]
    for mask in (4, 16, 2, 8, 1):
        more = lax.ppermute(mine, "band", [(p, p ^ mask) for p in range(n_band)])
        mine = jnp.concatenate([mine, more], axis=0)
        order = order + [r ^ mask for r in order]
    other = lax.ppermute(mine, "dom", [(d, d ^ 1) for d in range(n_dom)])

    rows = lax.all_to_all(
        filtered.reshape(n_band * n_dom, n_own, nz), ("band", "dom"), 0, 0, tiled=True
    ).reshape(n_all, nz)

    place = jnp.stack([band, core])
    rotated = rotate_kernel(n_band, order, n_mine, half, nz)(
        place, in_vmem(mine), in_vmem(other), in_vmem(rows)
    )
    rotated = lax.all_to_all(rotated.reshape(n_band, n_mine, nz), "band", 0, 0, tiled=True)
    rotated = rotated.transpose(1, 0, 2).astype(jnp.float32)
    return rotated.reshape(orbitals.shape)


def solution(mesh):
    in_specs = (P("band", "dom", None, None, None), P("dom", None, None, None), P(None, "band"))
    out_specs = P("band", "dom", None, None, None)
    return jax.shard_map(
        on_device, mesh=mesh, in_specs=in_specs, out_specs=out_specs, check_vma=False
    )
```

```python
import math

import jax
import jax.numpy as jnp
from jax import lax
from jax.experimental import pallas as pl
from jax.experimental.pallas import tpu as pltpu
from jax.sharding import PartitionSpec as P


DEG = 4

lower_bound = -1.5
cut_off = 1.0
upper_bound = 9.5
coef_zero = -2.5
coef_one = 4.0 / 3.0
coef_two = -1.0 / 12.0

PAD = 8


def filter_weights(degree):
    half_width = (upper_bound - cut_off) / 2.0
    centre = (upper_bound + cut_off) / 2.0
    sigma_now = half_width / (lower_bound - centre)
    first_scale = sigma_now / half_width
    inverse_gain = 2.0 / sigma_now
    weights = []
    for _ in range(1, degree):
        sigma_next = 1.0 / (inverse_gain - sigma_now)
        weights.append((2.0 * sigma_next / half_width, sigma_now * sigma_next))
        sigma_now = sigma_next
    return (centre, first_scale, weights)


def filter_kernel(n_dom, n_own, cx, cy, nz):
    side = math.isqrt(n_dom)
    gx, gy = side * cx, side * cy
    centre, first_scale, weights = filter_weights(DEG)
    row_stride = n_dom * n_own
    far_near = coef_two / coef_one

    def wrap(ref, band, x):
        ref[band, x, 0:PAD, :] = ref[band, x, gy : gy + PAD, :]
        ref[band, x, PAD + gy : PAD + gy + PAD, :] = ref[band, x, PAD : 2 * PAD, :]

    def shifted_ham(cur, diag, band, x):
        mid = cur[band, x, PAD : PAD + gy, :]

        def plane(step):
            return cur[band, lax.rem(x + (gx + step), gx), PAD : PAD + gy, :]

        def rows(step):
            return cur[band, x, PAD + step : PAD + step + gy, :]

        def lanes(step):
            return pltpu.roll(mid, step % nz, 1)

        near = (plane(-1) + plane(1)) + (rows(-1) + rows(1)) + (lanes(-1) + lanes(1))
        far = (plane(-2) + plane(2)) + (rows(-2) + rows(2)) + (lanes(-2) + lanes(2))
        return diag[x] * mid + (-0.5 * coef_one) * (near + far_near * far)

    def body(blocks, out, first, second, diag, ordered):
        def load(x, carry):
            for j in range(side):
                dom = lax.div(x, cx) * side + j
                inner = lax.rem(x, cx)
                for band in range(n_own):
                    first[band, x, PAD + j * cy : PAD + (j + 1) * cy, :] = blocks[
                        dom, band, inner
                    ].astype(jnp.float32)
                pot = blocks[dom, n_own, inner].astype(jnp.float32) + blocks[
                    dom, n_own + 1, inner
                ].astype(jnp.float32)
                diag[x, j * cy : (j + 1) * cy, :] = pot + (-1.5 * coef_zero - centre)
            for band in range(n_own):
                wrap(first, band, x)
            return carry

        lax.fori_loop(0, gx, load, 0)

        def run(step):
            def one(n, carry):
                step(lax.div(n, gx), lax.rem(n, gx))
                return carry

            lax.fori_loop(0, n_own * gx, one, 0)

        def start(band, x):
            second[band, x, PAD : PAD + gy, :] = shifted_ham(first, diag, band, x) * first_scale
            wrap(second, band, x)

        run(start)
        previous, current = first, second
        for scale_h, scale_x in weights[:-1]:

            def middle(band, x, previous=previous, current=current, scale_h=scale_h, scale_x=scale_x):
                following = shifted_ham(current, diag, band, x) * scale_h
                following = following - scale_x * previous[band, x, PAD : PAD + gy, :]
                previous[band, x, PAD : PAD + gy, :] = following
                wrap(previous, band, x)

            run(middle)
            previous, current = current, previous
        scale_h, scale_x = weights[-1]

        def last(band, x):
            following = shifted_ham(current, diag, band, x) * scale_h
            following = following - scale_x * previous[band, x, PAD : PAD + gy, :]
            for j in range(side):
                for part in range(cy // 8):
                    dom = lax.div(x, cx) * side + j
                    cell = lax.rem(x, cx) * cy + part * 8
                    base = cell * row_stride + dom * n_own + band
                    at = j * cy + part * 8
                    ordered[pl.ds(base, 8, stride=row_stride), :] = following[at : at + 8]

        run(last)
        block = 64

        def store(n, carry):
            at = pl.multiple_of(n * block, block)
            out[pl.ds(at, block), :] = ordered[pl.ds(at, block), :].astype(jnp.bfloat16)
            return carry

        lax.fori_loop(0, out.shape[0] // block, store, 0)

    padded = pltpu.VMEM((n_own, gx, gy + 2 * PAD, nz), jnp.float32)
    rows_out = cx * cy * n_dom * n_own
    return pl.pallas_call(
        body,
        out_shape=pltpu.VMEM((rows_out, nz), jnp.bfloat16),
        in_specs=[pl.BlockSpec(memory_space=pltpu.VMEM)],
        out_specs=pl.BlockSpec(memory_space=pltpu.VMEM),
        scratch_shapes=[
            padded,
            padded,
            pltpu.VMEM((gx, gy, nz), jnp.float32),
            pltpu.VMEM((rows_out, nz), jnp.float32),
        ],
        name="chebyshev",
    )


def rotate_kernel(n_all, n_x, piece, nz):
    def body(place, mine, other, rows, out):
        core, x = place[0], place[1]

        def half(pieces, which):
            left = jnp.concatenate([pieces[r] for r in range(n_x)], axis=1)
            right = []
            for r in range(n_x):
                q = which * n_x + lax.rem(x + r, n_x)
                right.append(rows[pl.ds(pl.multiple_of(q * piece, piece), piece), :])
            right = jnp.concatenate(right, axis=0)
            return jnp.dot(left, right, preferred_element_type=jnp.float32)

        out[...] = (half(mine, core) + half(other, 1 - core)).astype(jnp.bfloat16)

    vmem = pl.BlockSpec(memory_space=pltpu.VMEM)
    return pl.pallas_call(
        body,
        out_shape=pltpu.VMEM((n_all, nz), jnp.bfloat16),
        in_specs=[pl.BlockSpec(memory_space=pltpu.SMEM), vmem, vmem, vmem],
        out_specs=vmem,
        name="rotate",
    )


def in_vmem(x):
    return pltpu.with_memory_space_constraint(x, pltpu.VMEM)


def on_device(orbitals, potential, ritz):
    n_dom = lax.axis_size("dom")
    n_band = lax.axis_size("band")
    n_mine, _, cx, cy, nz = orbitals.shape
    n_all = ritz.shape[0]
    n_own = n_mine // n_dom
    n_x = n_dom // 4
    dom = lax.axis_index("dom")
    core = lax.rem(dom, 2)
    x = lax.rem(lax.div(dom, 2), n_x)

    pot = potential[0]
    high = lax.reduce_precision(pot, 8, 7)
    parts = jnp.stack([high, pot - high]).astype(jnp.bfloat16)
    parts = jnp.broadcast_to(parts[None], (n_dom, 2, cx, cy, nz))
    blocks = orbitals.reshape(n_dom, n_own, cx, cy, nz)
    blocks = jnp.concatenate([blocks, parts], axis=1)
    blocks = lax.all_to_all(blocks, "dom", 0, 0, tiled=True)
    filtered = filter_kernel(n_dom, n_own, cx, cy, nz)(in_vmem(blocks))

    piece = n_all // (2 * n_x)
    own = lax.dynamic_slice_in_dim(ritz.T, (core * n_x + x) * piece, piece, 1)
    many = jnp.broadcast_to(own[None], (n_band,) + own.shape)

    def from_x(value, step):
        pairs = []
        for d in range(n_dom):
            z, at, c = d // (2 * n_x), d // 2 % n_x, d % 2
            pairs.append((z * 2 * n_x + (at + step) % n_x * 2 + c, d))
        return lax.ppermute(value, "dom", pairs)

    own = lax.all_to_all(many, "band", 0, 0, tiled=True).reshape(n_all, piece)
    after = from_x(own, 1)
    before = from_x(own, -1)
    far = from_x(after, 1)
    mine = jnp.stack([own, after, far, before])
    other = lax.ppermute(mine, "dom", [(d, d ^ 1) for d in range(n_dom)])

    rows = lax.all_to_all(
        filtered.reshape(n_band * n_dom, n_own, nz), ("band", "dom"), 0, 0, tiled=True
    ).reshape(n_all, nz)

    place = jnp.stack([core, x])
    rotated = rotate_kernel(n_all, n_x, piece, nz)(
        place, in_vmem(mine), in_vmem(other), in_vmem(rows)
    )
    rotated = lax.all_to_all(rotated.reshape(n_band, n_mine, nz), "band", 0, 0, tiled=True)
    rotated = rotated.transpose(1, 0, 2).astype(jnp.float32)
    return rotated.reshape(orbitals.shape)


def solution(mesh):
    in_specs = (P("band", "dom", None, None, None), P("dom", None, None, None), P(None, "band"))
    out_specs = P("band", "dom", None, None, None)
    return jax.shard_map(
        on_device, mesh=mesh, in_specs=in_specs, out_specs=out_specs, check_vma=False
    )
```

```python
import math

import jax
import jax.numpy as jnp
from jax import lax
from jax.experimental import pallas as pl
from jax.experimental.pallas import tpu as pltpu
from jax.sharding import PartitionSpec as P


DEG = 4

lower_bound = -1.5
cut_off = 1.0
upper_bound = 9.5
coef_zero = -2.5
coef_one = 4.0 / 3.0
coef_two = -1.0 / 12.0

PAD = 8


def filter_weights(degree):
    half_width = (upper_bound - cut_off) / 2.0
    centre = (upper_bound + cut_off) / 2.0
    sigma_now = half_width / (lower_bound - centre)
    first_scale = sigma_now / half_width
    inverse_gain = 2.0 / sigma_now
    weights = []
    for _ in range(1, degree):
        sigma_next = 1.0 / (inverse_gain - sigma_now)
        weights.append((2.0 * sigma_next / half_width, sigma_now * sigma_next))
        sigma_now = sigma_next
    return (centre, first_scale, weights)


def filter_kernel(n_dom, n_own, cx, cy, nz):
    side = math.isqrt(n_dom)
    gx, gy = side * cx, side * cy
    centre, first_scale, weights = filter_weights(DEG)
    row_stride = n_dom * n_own
    far_near = coef_two / coef_one

    def wrap(ref, band, x):
        ref[band, x, 0:PAD, :] = ref[band, x, gy : gy + PAD, :]
        ref[band, x, PAD + gy : PAD + gy + PAD, :] = ref[band, x, PAD : 2 * PAD, :]

    def shifted_ham(cur, diag, band, x):
        mid = cur[band, x, PAD : PAD + gy, :]

        def plane(step):
            return cur[band, lax.rem(x + (gx + step), gx), PAD : PAD + gy, :]

        def rows(step):
            return cur[band, x, PAD + step : PAD + step + gy, :]

        def lanes(step):
            return pltpu.roll(mid, step % nz, 1)

        near = (plane(-1) + plane(1)) + (rows(-1) + rows(1)) + (lanes(-1) + lanes(1))
        far = (plane(-2) + plane(2)) + (rows(-2) + rows(2)) + (lanes(-2) + lanes(2))
        return diag[x] * mid + (-0.5 * coef_one) * (near + far_near * far)

    def body(blocks, out, first, second, diag, ordered):
        def load(x, carry):
            for j in range(side):
                dom = lax.div(x, cx) * side + j
                inner = lax.rem(x, cx)
                for band in range(n_own):
                    first[band, x, PAD + j * cy : PAD + (j + 1) * cy, :] = blocks[
                        dom, band, inner
                    ].astype(jnp.float32)
                pot = blocks[dom, n_own, inner].astype(jnp.float32) + blocks[
                    dom, n_own + 1, inner
                ].astype(jnp.float32)
                diag[x, j * cy : (j + 1) * cy, :] = pot + (-1.5 * coef_zero - centre)
            for band in range(n_own):
                wrap(first, band, x)
            return carry

        lax.fori_loop(0, gx, load, 0)

        def run(step):
            def one(n, carry):
                step(lax.div(n, gx), lax.rem(n, gx))
                return carry

            lax.fori_loop(0, n_own * gx, one, 0)

        def start(band, x):
            second[band, x, PAD : PAD + gy, :] = shifted_ham(first, diag, band, x) * first_scale
            wrap(second, band, x)

        run(start)
        previous, current = first, second
        for scale_h, scale_x in weights[:-1]:

            def middle(band, x, previous=previous, current=current, scale_h=scale_h, scale_x=scale_x):
                following = shifted_ham(current, diag, band, x) * scale_h
                following = following - scale_x * previous[band, x, PAD : PAD + gy, :]
                previous[band, x, PAD : PAD + gy, :] = following
                wrap(previous, band, x)

            run(middle)
            previous, current = current, previous
        scale_h, scale_x = weights[-1]

        def last(band, x):
            following = shifted_ham(current, diag, band, x) * scale_h
            following = following - scale_x * previous[band, x, PAD : PAD + gy, :]
            for j in range(side):
                for part in range(cy // 8):
                    dom = lax.div(x, cx) * side + j
                    cell = lax.rem(x, cx) * cy + part * 8
                    base = cell * row_stride + dom * n_own + band
                    at = j * cy + part * 8
                    ordered[pl.ds(base, 8, stride=row_stride), :] = following[at : at + 8]

        run(last)
        block = 64

        def store(n, carry):
            at = pl.multiple_of(n * block, block)
            out[pl.ds(at, block), :] = ordered[pl.ds(at, block), :].astype(jnp.bfloat16)
            return carry

        lax.fori_loop(0, out.shape[0] // block, store, 0)

    padded = pltpu.VMEM((n_own, gx, gy + 2 * PAD, nz), jnp.float32)
    rows_out = cx * cy * n_dom * n_own
    return pl.pallas_call(
        body,
        out_shape=pltpu.VMEM((rows_out, nz), jnp.bfloat16),
        in_specs=[pl.BlockSpec(memory_space=pltpu.VMEM)],
        out_specs=pl.BlockSpec(memory_space=pltpu.VMEM),
        scratch_shapes=[
            padded,
            padded,
            pltpu.VMEM((gx, gy, nz), jnp.float32),
            pltpu.VMEM((rows_out, nz), jnp.float32),
        ],
        name="chebyshev",
    )


def rotate_kernel(n_all, n_x, nz):
    half, block = n_all // 2, n_all // n_x

    def body(mine, other, rows, out):
        core, x = chip_place(n_x)
        near = rows[pl.ds(pl.multiple_of(core * half, half), half), :]
        far = rows[pl.ds(pl.multiple_of((1 - core) * half, half), half), :]
        for r in range(n_x):
            sums = jnp.dot(mine[r], near, preferred_element_type=jnp.float32)
            sums = sums + jnp.dot(other[r], far, preferred_element_type=jnp.float32)
            at = pl.multiple_of(lax.rem(x + r, n_x) * block, block)
            out[pl.ds(at, block), :] = sums.astype(jnp.bfloat16)

    vmem = pl.BlockSpec(memory_space=pltpu.VMEM)
    return pl.pallas_call(
        body,
        out_shape=pltpu.VMEM((n_all, nz), jnp.bfloat16),
        in_specs=[vmem, vmem, vmem],
        out_specs=vmem,
        name="rotate",
    )


def chip_place(n_x):
    dom = lax.axis_index("dom")
    return lax.rem(dom, 2), lax.rem(lax.div(dom, 2), n_x)


def in_vmem(x):
    return pltpu.with_memory_space_constraint(x, pltpu.VMEM)


def on_device(orbitals, potential, ritz):
    n_dom = lax.axis_size("dom")
    n_band = lax.axis_size("band")
    n_mine, _, cx, cy, nz = orbitals.shape
    n_all = ritz.shape[0]
    n_own = n_mine // n_dom
    n_x = n_dom // 4
    n_y = n_band // n_x
    core, _ = chip_place(n_x)

    pot = potential[0]
    high = lax.reduce_precision(pot, 8, 7)
    parts = jnp.stack([high, pot - high]).astype(jnp.bfloat16)
    parts = jnp.broadcast_to(parts[None], (n_dom, 2, cx, cy, nz))
    blocks = orbitals.reshape(n_dom, n_own, cx, cy, nz)
    blocks = jnp.concatenate([blocks, parts], axis=1)
    blocks = lax.all_to_all(blocks, "dom", 0, 0, tiled=True)
    filtered = filter_kernel(n_dom, n_own, cx, cy, nz)(in_vmem(blocks))

    half = n_all // 2

    def split(d):
        return d // (2 * n_x), d // 2 % n_x, d % 2

    def from_x(value, step):
        pairs = []
        for d in range(n_dom):
            z, x, c = split(d)
            pairs.append((z * 2 * n_x + (x + step) % n_x * 2 + c, d))
        return lax.ppermute(value, "dom", pairs)

    turned = []
    for d in range(n_dom):
        z, x, c = split(d)
        for p in range(n_band):
            high_z, y = p // n_y, p % n_y
            source = (z * 2 * n_x + high_z * 2 + c) * n_band + x * n_y + y
            turned.append((source, d * n_band + p))

    own = lax.dynamic_slice_in_dim(ritz.T, core * half, half, 1)
    own = lax.ppermute(own, ("dom", "band"), turned)
    many = jnp.broadcast_to(own[None], (n_y,) + own.shape)
    lines = [[z * n_y + y for y in range(n_y)] for z in range(n_x)]
    own = lax.all_to_all(many, "band", 0, 0, tiled=True, axis_index_groups=lines)
    own = own.reshape(n_y * n_mine, half)
    after = from_x(own, 1)
    before = from_x(own, -1)
    far = from_x(own, 2)
    mine = jnp.stack([own, after, far, before])
    other = lax.ppermute(mine, "dom", [(d, d ^ 1) for d in range(n_dom)])

    rows = lax.all_to_all(
        filtered.reshape(n_band * n_dom, n_own, nz), ("band", "dom"), 0, 0, tiled=True
    ).reshape(n_all, nz)

    rotated = rotate_kernel(n_all, n_x, nz)(in_vmem(mine), in_vmem(other), in_vmem(rows))
    rotated = lax.all_to_all(rotated.reshape(n_band, n_mine, nz), "band", 0, 0, tiled=True)
    rotated = rotated.transpose(1, 0, 2).astype(jnp.float32)
    return rotated.reshape(orbitals.shape)


def solution(mesh):
    in_specs = (P("band", "dom", None, None, None), P("dom", None, None, None), P(None, "band"))
    out_specs = P("band", "dom", None, None, None)
    return jax.shard_map(
        on_device, mesh=mesh, in_specs=in_specs, out_specs=out_specs, check_vma=False
    )
```

```python
import math

import jax
import jax.numpy as jnp
from jax import lax
from jax.experimental import pallas as pl
from jax.experimental.pallas import tpu as pltpu
from jax.sharding import PartitionSpec as P


DEG = 4

lower_bound = -1.5
cut_off = 1.0
upper_bound = 9.5
coef_zero = -2.5
coef_one = 4.0 / 3.0
coef_two = -1.0 / 12.0

PAD = 8


def filter_weights(degree):
    half_width = (upper_bound - cut_off) / 2.0
    centre = (upper_bound + cut_off) / 2.0
    sigma_now = half_width / (lower_bound - centre)
    first_scale = sigma_now / half_width
    inverse_gain = 2.0 / sigma_now
    weights = []
    for _ in range(1, degree):
        sigma_next = 1.0 / (inverse_gain - sigma_now)
        weights.append((2.0 * sigma_next / half_width, sigma_now * sigma_next))
        sigma_now = sigma_next
    return (centre, first_scale, weights)


def filter_kernel(n_dom, n_own, cx, cy, nz):
    side = math.isqrt(n_dom)
    gx, gy = side * cx, side * cy
    centre, first_scale, weights = filter_weights(DEG)
    row_stride = n_dom * n_own
    far_near = coef_two / coef_one

    def wrap(ref, band, x):
        ref[band, x, 0:PAD, :] = ref[band, x, gy : gy + PAD, :]
        ref[band, x, PAD + gy : PAD + gy + PAD, :] = ref[band, x, PAD : 2 * PAD, :]

    def shifted_ham(cur, diag, band, x):
        mid = cur[band, x, PAD : PAD + gy, :]

        def plane(step):
            return cur[band, lax.rem(x + (gx + step), gx), PAD : PAD + gy, :]

        def rows(step):
            return cur[band, x, PAD + step : PAD + step + gy, :]

        def lanes(step):
            return pltpu.roll(mid, step % nz, 1)

        near = (plane(-1) + plane(1)) + (rows(-1) + rows(1)) + (lanes(-1) + lanes(1))
        far = (plane(-2) + plane(2)) + (rows(-2) + rows(2)) + (lanes(-2) + lanes(2))
        return diag[x] * mid + (-0.5 * coef_one) * (near + far_near * far)

    def body(blocks, out, first, second, diag, ordered):
        def load(x, carry):
            for j in range(side):
                dom = lax.div(x, cx) * side + j
                inner = lax.rem(x, cx)
                for band in range(n_own):
                    first[band, x, PAD + j * cy : PAD + (j + 1) * cy, :] = blocks[
                        dom, band, inner
                    ].astype(jnp.float32)
                pot = blocks[dom, n_own, inner].astype(jnp.float32) + blocks[
                    dom, n_own + 1, inner
                ].astype(jnp.float32)
                diag[x, j * cy : (j + 1) * cy, :] = pot + (-1.5 * coef_zero - centre)
            for band in range(n_own):
                wrap(first, band, x)
            return carry

        lax.fori_loop(0, gx, load, 0)

        def run(step):
            def one(n, carry):
                step(lax.div(n, gx), lax.rem(n, gx))
                return carry

            lax.fori_loop(0, n_own * gx, one, 0)

        def start(band, x):
            second[band, x, PAD : PAD + gy, :] = shifted_ham(first, diag, band, x) * first_scale
            wrap(second, band, x)

        run(start)
        previous, current = first, second
        for scale_h, scale_x in weights[:-1]:

            def middle(band, x, previous=previous, current=current, scale_h=scale_h, scale_x=scale_x):
                following = shifted_ham(current, diag, band, x) * scale_h
                following = following - scale_x * previous[band, x, PAD : PAD + gy, :]
                previous[band, x, PAD : PAD + gy, :] = following
                wrap(previous, band, x)

            run(middle)
            previous, current = current, previous
        scale_h, scale_x = weights[-1]

        def last(band, x):
            following = shifted_ham(current, diag, band, x) * scale_h
            following = following - scale_x * previous[band, x, PAD : PAD + gy, :]
            for j in range(side):
                for part in range(cy // 8):
                    dom = lax.div(x, cx) * side + j
                    cell = lax.rem(x, cx) * cy + part * 8
                    base = cell * row_stride + dom * n_own + band
                    at = j * cy + part * 8
                    ordered[pl.ds(base, 8, stride=row_stride), :] = following[at : at + 8]

        run(last)
        block = 64

        def store(n, carry):
            at = pl.multiple_of(n * block, block)
            out[pl.ds(at, block), :] = ordered[pl.ds(at, block), :].astype(jnp.bfloat16)
            return carry

        lax.fori_loop(0, out.shape[0] // block, store, 0)

    padded = pltpu.VMEM((n_own, gx, gy + 2 * PAD, nz), jnp.float32)
    rows_out = cx * cy * n_dom * n_own
    return pl.pallas_call(
        body,
        out_shape=pltpu.VMEM((rows_out, nz), jnp.bfloat16),
        in_specs=[pl.BlockSpec(memory_space=pltpu.VMEM)],
        out_specs=pl.BlockSpec(memory_space=pltpu.VMEM),
        scratch_shapes=[
            padded,
            padded,
            pltpu.VMEM((gx, gy, nz), jnp.float32),
            pltpu.VMEM((rows_out, nz), jnp.float32),
        ],
        name="chebyshev",
    )


def rotate_kernel(n_all, n_x, nz):
    piece = n_all // (2 * n_x)
    block = 256

    def body(mine, other, rows, out):
        core, x = chip_place(n_x)
        right = []
        for which in (core, 1 - core):
            for r in range(n_x):
                q = which * n_x + lax.rem(x + r, n_x)
                right.append(rows[pl.ds(pl.multiple_of(q * piece, piece), piece), :])
        right = jnp.concatenate(right, axis=0)
        for at in range(0, n_all, block):
            left = [p[r, at : at + block, :] for p in (mine, other) for r in range(n_x)]
            left = jnp.concatenate(left, axis=1)
            sums = jnp.dot(left, right, preferred_element_type=jnp.float32)
            out[at : at + block, :] = sums.astype(jnp.bfloat16)

    vmem = pl.BlockSpec(memory_space=pltpu.VMEM)
    return pl.pallas_call(
        body,
        out_shape=pltpu.VMEM((n_all, nz), jnp.bfloat16),
        in_specs=[vmem, vmem, vmem],
        out_specs=vmem,
        name="rotate",
    )


def chip_place(n_x):
    dom = lax.axis_index("dom")
    return lax.rem(dom, 2), lax.rem(lax.div(dom, 2), n_x)


def in_vmem(x):
    return pltpu.with_memory_space_constraint(x, pltpu.VMEM)


def on_device(orbitals, potential, ritz):
    n_dom = lax.axis_size("dom")
    n_band = lax.axis_size("band")
    n_mine, _, cx, cy, nz = orbitals.shape
    n_all = ritz.shape[0]
    n_own = n_mine // n_dom
    n_x = n_dom // 4
    core, x = chip_place(n_x)

    pot = potential[0]
    high = lax.reduce_precision(pot, 8, 7)
    parts = jnp.stack([high, pot - high]).astype(jnp.bfloat16)
    parts = jnp.broadcast_to(parts[None], (n_dom, 2, cx, cy, nz))
    blocks = orbitals.reshape(n_dom, n_own, cx, cy, nz)
    blocks = jnp.concatenate([blocks, parts], axis=1)
    blocks = lax.all_to_all(blocks, "dom", 0, 0, tiled=True)
    filtered = filter_kernel(n_dom, n_own, cx, cy, nz)(in_vmem(blocks))

    piece = n_all // (2 * n_x)
    own = lax.dynamic_slice_in_dim(ritz.T, (core * n_x + x) * piece, piece, 1)
    many = jnp.broadcast_to(own[None], (n_band,) + own.shape)

    def from_x(value, step):
        pairs = []
        for d in range(n_dom):
            z, at, c = d // (2 * n_x), d // 2 % n_x, d % 2
            pairs.append((z * 2 * n_x + (at + step) % n_x * 2 + c, d))
        return lax.ppermute(value, "dom", pairs)

    own = lax.all_to_all(many, "band", 0, 0, tiled=True).reshape(n_all, piece)
    after = from_x(own, 1)
    before = from_x(own, -1)
    far = from_x(own, 2)
    mine = jnp.stack([own, after, far, before])
    other = lax.ppermute(mine, "dom", [(d, d ^ 1) for d in range(n_dom)])

    rows = lax.all_to_all(
        filtered.reshape(n_band * n_dom, n_own, nz), ("band", "dom"), 0, 0, tiled=True
    ).reshape(n_all, nz)

    rotated = rotate_kernel(n_all, n_x, nz)(in_vmem(mine), in_vmem(other), in_vmem(rows))
    rotated = lax.all_to_all(rotated.reshape(n_band, n_mine, nz), "band", 0, 0, tiled=True)
    rotated = rotated.transpose(1, 0, 2).astype(jnp.float32)
    return rotated.reshape(orbitals.shape)


def solution(mesh):
    in_specs = (P("band", "dom", None, None, None), P("dom", None, None, None), P(None, "band"))
    out_specs = P("band", "dom", None, None, None)
    return jax.shard_map(
        on_device, mesh=mesh, in_specs=in_specs, out_specs=out_specs, check_vma=False
    )
```

```python
import math

import jax
import jax.numpy as jnp
from jax import lax
from jax.experimental import pallas as pl
from jax.experimental.pallas import tpu as pltpu
from jax.sharding import PartitionSpec as P


DEG = 4

lower_bound = -1.5
cut_off = 1.0
upper_bound = 9.5
coef_zero = -2.5
coef_one = 4.0 / 3.0
coef_two = -1.0 / 12.0

PAD = 8


def filter_weights(degree):
    half_width = (upper_bound - cut_off) / 2.0
    centre = (upper_bound + cut_off) / 2.0
    sigma_now = half_width / (lower_bound - centre)
    first_scale = sigma_now / half_width
    inverse_gain = 2.0 / sigma_now
    weights = []
    for _ in range(1, degree):
        sigma_next = 1.0 / (inverse_gain - sigma_now)
        weights.append((2.0 * sigma_next / half_width, sigma_now * sigma_next))
        sigma_now = sigma_next
    return (centre, first_scale, weights)


def filter_kernel(n_dom, n_own, cx, cy, nz):
    side = math.isqrt(n_dom)
    gx, gy = side * cx, side * cy
    centre, first_scale, weights = filter_weights(DEG)
    row_stride = n_dom * n_own
    far_near = coef_two / coef_one

    def wrap(ref, band, x):
        ref[band, x, 0:PAD, :] = ref[band, x, gy : gy + PAD, :]
        ref[band, x, PAD + gy : PAD + gy + PAD, :] = ref[band, x, PAD : 2 * PAD, :]

    def shifted_ham(cur, diag, band, x):
        mid = cur[band, x, PAD : PAD + gy, :]

        def plane(step):
            return cur[band, lax.rem(x + (gx + step), gx), PAD : PAD + gy, :]

        def rows(step):
            return cur[band, x, PAD + step : PAD + step + gy, :]

        def lanes(step):
            return pltpu.roll(mid, step % nz, 1)

        near = (plane(-1) + plane(1)) + (rows(-1) + rows(1)) + (lanes(-1) + lanes(1))
        far = (plane(-2) + plane(2)) + (rows(-2) + rows(2)) + (lanes(-2) + lanes(2))
        return diag[x] * mid + (-0.5 * coef_one) * (near + far_near * far)

    def body(blocks, out, first, second, diag, ordered):
        def load(x, carry):
            for j in range(side):
                dom = lax.div(x, cx) * side + j
                inner = lax.rem(x, cx)
                for band in range(n_own):
                    first[band, x, PAD + j * cy : PAD + (j + 1) * cy, :] = blocks[
                        dom, band, inner
                    ].astype(jnp.float32)
                pot = blocks[dom, n_own, inner].astype(jnp.float32) + blocks[
                    dom, n_own + 1, inner
                ].astype(jnp.float32)
                diag[x, j * cy : (j + 1) * cy, :] = pot + (-1.5 * coef_zero - centre)
            for band in range(n_own):
                wrap(first, band, x)
            return carry

        lax.fori_loop(0, gx, load, 0)

        def run(step):
            def one(n, carry):
                step(lax.div(n, gx), lax.rem(n, gx))
                return carry

            lax.fori_loop(0, n_own * gx, one, 0)

        def start(band, x):
            second[band, x, PAD : PAD + gy, :] = shifted_ham(first, diag, band, x) * first_scale
            wrap(second, band, x)

        run(start)
        previous, current = first, second
        for scale_h, scale_x in weights[:-1]:

            def middle(band, x, previous=previous, current=current, scale_h=scale_h, scale_x=scale_x):
                following = shifted_ham(current, diag, band, x) * scale_h
                following = following - scale_x * previous[band, x, PAD : PAD + gy, :]
                previous[band, x, PAD : PAD + gy, :] = following
                wrap(previous, band, x)

            run(middle)
            previous, current = current, previous
        scale_h, scale_x = weights[-1]

        def last(band, x):
            following = shifted_ham(current, diag, band, x) * scale_h
            following = following - scale_x * previous[band, x, PAD : PAD + gy, :]
            for j in range(side):
                for part in range(cy // 8):
                    dom = lax.div(x, cx) * side + j
                    cell = lax.rem(x, cx) * cy + part * 8
                    base = cell * row_stride + dom * n_own + band
                    at = j * cy + part * 8
                    ordered[pl.ds(base, 8, stride=row_stride), :] = following[at : at + 8]

        run(last)
        block = 64

        def store(n, carry):
            at = pl.multiple_of(n * block, block)
            out[pl.ds(at, block), :] = ordered[pl.ds(at, block), :].astype(jnp.bfloat16)
            return carry

        lax.fori_loop(0, out.shape[0] // block, store, 0)

    padded = pltpu.VMEM((n_own, gx, gy + 2 * PAD, nz), jnp.float32)
    rows_out = cx * cy * n_dom * n_own
    return pl.pallas_call(
        body,
        out_shape=pltpu.VMEM((rows_out, nz), jnp.bfloat16),
        in_specs=[pl.BlockSpec(memory_space=pltpu.VMEM)],
        out_specs=pl.BlockSpec(memory_space=pltpu.VMEM),
        scratch_shapes=[
            padded,
            padded,
            pltpu.VMEM((gx, gy, nz), jnp.float32),
            pltpu.VMEM((rows_out, nz), jnp.float32),
        ],
        name="chebyshev",
    )


def rotate_kernel(n_all, n_x, nz):
    half, block = n_all // 2, n_all // n_x

    def body(mine, other, rows, out):
        core, x = chip_place(n_x)
        first = lax.div(lax.axis_index("band"), lax.axis_size("band") // n_x) + x
        near = rows[pl.ds(pl.multiple_of(core * half, half), half), :]
        far = rows[pl.ds(pl.multiple_of((1 - core) * half, half), half), :]
        for r in range(n_x):
            sums = jnp.dot(mine[r], near, preferred_element_type=jnp.float32)
            sums = sums + jnp.dot(other[r], far, preferred_element_type=jnp.float32)
            at = pl.multiple_of(lax.rem(first + r, n_x) * block, block)
            out[pl.ds(at, block), :] = sums.astype(jnp.bfloat16)

    vmem = pl.BlockSpec(memory_space=pltpu.VMEM)
    return pl.pallas_call(
        body,
        out_shape=pltpu.VMEM((n_all, nz), jnp.bfloat16),
        in_specs=[vmem, vmem, vmem],
        out_specs=vmem,
        name="rotate",
    )


def chip_place(n_x):
    dom = lax.axis_index("dom")
    return lax.rem(dom, 2), lax.rem(lax.div(dom, 2), n_x)


def in_vmem(x):
    return pltpu.with_memory_space_constraint(x, pltpu.VMEM)


def on_device(orbitals, potential, ritz):
    n_dom = lax.axis_size("dom")
    n_band = lax.axis_size("band")
    n_mine, _, cx, cy, nz = orbitals.shape
    n_all = ritz.shape[0]
    n_own = n_mine // n_dom
    n_x = n_dom // 4
    n_y = n_band // n_x
    core, _ = chip_place(n_x)

    pot = potential[0]
    high = lax.reduce_precision(pot, 8, 7)
    parts = jnp.stack([high, pot - high]).astype(jnp.bfloat16)
    parts = jnp.broadcast_to(parts[None], (n_dom, 2, cx, cy, nz))
    blocks = orbitals.reshape(n_dom, n_own, cx, cy, nz)
    blocks = jnp.concatenate([blocks, parts], axis=1)
    blocks = lax.all_to_all(blocks, "dom", 0, 0, tiled=True)
    filtered = filter_kernel(n_dom, n_own, cx, cy, nz)(in_vmem(blocks))

    half = n_all // 2

    def split(d):
        return d // (2 * n_x), d // 2 % n_x, d % 2

    def from_x(value, step):
        pairs = []
        for d in range(n_dom):
            z, x, c = split(d)
            pairs.append((z * 2 * n_x + (x + step) % n_x * 2 + c, d))
        return lax.ppermute(value, "dom", pairs)

    turned = []
    for d in range(n_dom):
        z, x, c = split(d)
        for p in range(n_band):
            high_z, y = p // n_y, p % n_y
            near_z = 1 - z if x == 2 else z
            source = (near_z * 2 * n_x + x * 2 + c) * n_band + (high_z + x) % n_x * n_y + y
            turned.append((source, d * n_band + p))

    own = lax.dynamic_slice_in_dim(ritz.T, core * half, half, 1)
    own = lax.ppermute(own, ("dom", "band"), turned)
    many = jnp.broadcast_to(own[None], (n_y,) + own.shape)
    lines = [[z * n_y + y for y in range(n_y)] for z in range(n_x)]
    own = lax.all_to_all(many, "band", 0, 0, tiled=True, axis_index_groups=lines)
    own = own.reshape(n_y * n_mine, half)
    after = from_x(own, 1)
    before = from_x(own, -1)
    far = from_x(own, 2)
    mine = jnp.stack([own, after, far, before])
    other = lax.ppermute(mine, "dom", [(d, d ^ 1) for d in range(n_dom)])

    rows = lax.all_to_all(
        filtered.reshape(n_band * n_dom, n_own, nz), ("band", "dom"), 0, 0, tiled=True
    ).reshape(n_all, nz)

    rotated = rotate_kernel(n_all, n_x, nz)(in_vmem(mine), in_vmem(other), in_vmem(rows))
    rotated = lax.all_to_all(rotated.reshape(n_band, n_mine, nz), "band", 0, 0, tiled=True)
    rotated = rotated.transpose(1, 0, 2).astype(jnp.float32)
    return rotated.reshape(orbitals.shape)


def solution(mesh):
    in_specs = (P("band", "dom", None, None, None), P("dom", None, None, None), P(None, "band"))
    out_specs = P("band", "dom", None, None, None)
    return jax.shard_map(
        on_device, mesh=mesh, in_specs=in_specs, out_specs=out_specs, check_vma=False
    )
```

```python
import math

import jax
import jax.numpy as jnp
from jax import lax
from jax.experimental import pallas as pl
from jax.experimental.pallas import tpu as pltpu
from jax.sharding import PartitionSpec as P


DEG = 4

lower_bound = -1.5
cut_off = 1.0
upper_bound = 9.5
coef_zero = -2.5
coef_one = 4.0 / 3.0
coef_two = -1.0 / 12.0

PAD = 8


def filter_weights(degree):
    half_width = (upper_bound - cut_off) / 2.0
    centre = (upper_bound + cut_off) / 2.0
    sigma_now = half_width / (lower_bound - centre)
    first_scale = sigma_now / half_width
    inverse_gain = 2.0 / sigma_now
    weights = []
    for _ in range(1, degree):
        sigma_next = 1.0 / (inverse_gain - sigma_now)
        weights.append((2.0 * sigma_next / half_width, sigma_now * sigma_next))
        sigma_now = sigma_next
    return (centre, first_scale, weights)


def filter_kernel(n_dom, n_own, cx, cy, nz):
    side = math.isqrt(n_dom)
    gx, gy = side * cx, side * cy
    centre, first_scale, weights = filter_weights(DEG)
    row_stride = n_dom // 2 * n_own
    rows_out = cx * cy * row_stride
    far_near = coef_two / coef_one

    def wrap(ref, band, x):
        ref[band, x, 0:PAD, :] = ref[band, x, gy : gy + PAD, :]
        ref[band, x, PAD + gy : PAD + gy + PAD, :] = ref[band, x, PAD : 2 * PAD, :]

    def shifted_ham(cur, diag, band, x):
        mid = cur[band, x, PAD : PAD + gy, :]

        def plane(step):
            return cur[band, lax.rem(x + (gx + step), gx), PAD : PAD + gy, :]

        def rows(step):
            return cur[band, x, PAD + step : PAD + step + gy, :]

        def lanes(step):
            return pltpu.roll(mid, step % nz, 1)

        near = (plane(-1) + plane(1)) + (rows(-1) + rows(1)) + (lanes(-1) + lanes(1))
        far = (plane(-2) + plane(2)) + (rows(-2) + rows(2)) + (lanes(-2) + lanes(2))
        return diag[x] * mid + (-0.5 * coef_one) * (near + far_near * far)

    def body(blocks, out, away, first, second, diag, ordered):
        core, _ = chip_place(side)

        def load(x, carry):
            for j in range(side):
                dom = lax.div(x, cx) * side + j
                inner = lax.rem(x, cx)
                for band in range(n_own):
                    first[band, x, PAD + j * cy : PAD + (j + 1) * cy, :] = blocks[
                        dom, band, inner
                    ].astype(jnp.float32)
                pot = blocks[dom, n_own, inner].astype(jnp.float32) + blocks[
                    dom, n_own + 1, inner
                ].astype(jnp.float32)
                diag[x, j * cy : (j + 1) * cy, :] = pot + (-1.5 * coef_zero - centre)
            for band in range(n_own):
                wrap(first, band, x)
            return carry

        lax.fori_loop(0, gx, load, 0)

        def run(step):
            def one(n, carry):
                step(lax.div(n, gx), lax.rem(n, gx))
                return carry

            lax.fori_loop(0, n_own * gx, one, 0)

        def start(band, x):
            second[band, x, PAD : PAD + gy, :] = shifted_ham(first, diag, band, x) * first_scale
            wrap(second, band, x)

        run(start)
        previous, current = first, second
        for scale_h, scale_x in weights[:-1]:

            def middle(band, x, previous=previous, current=current, scale_h=scale_h, scale_x=scale_x):
                following = shifted_ham(current, diag, band, x) * scale_h
                following = following - scale_x * previous[band, x, PAD : PAD + gy, :]
                previous[band, x, PAD : PAD + gy, :] = following
                wrap(previous, band, x)

            run(middle)
            previous, current = current, previous
        scale_h, scale_x = weights[-1]

        def last(band, x):
            following = shifted_ham(current, diag, band, x) * scale_h
            following = following - scale_x * previous[band, x, PAD : PAD + gy, :]
            for j in range(side):
                for part in range(cy // 8):
                    pair = lax.div(x, cx) * (side // 2) + j // 2
                    cell = lax.rem(x, cx) * cy + part * 8
                    base = cell * row_stride + pair * n_own + band
                    base = base + lax.bitwise_xor(core, j % 2) * rows_out
                    at = j * cy + part * 8
                    ordered[pl.ds(base, 8, stride=row_stride), :] = following[at : at + 8]

        run(last)
        block = 64

        def store(n, carry):
            at = pl.multiple_of(n * block, block)
            out[pl.ds(at, block), :] = ordered[pl.ds(at, block), :].astype(jnp.bfloat16)
            far = ordered[pl.ds(rows_out + at, block), :]
            away[pl.ds(at, block), :] = far.astype(jnp.bfloat16)
            return carry

        lax.fori_loop(0, out.shape[0] // block, store, 0)

    padded = pltpu.VMEM((n_own, gx, gy + 2 * PAD, nz), jnp.float32)
    vmem = pl.BlockSpec(memory_space=pltpu.VMEM)
    return pl.pallas_call(
        body,
        out_shape=[pltpu.VMEM((rows_out, nz), jnp.bfloat16)] * 2,
        in_specs=[vmem],
        out_specs=[vmem, vmem],
        scratch_shapes=[
            padded,
            padded,
            pltpu.VMEM((gx, gy, nz), jnp.float32),
            pltpu.VMEM((2 * rows_out, nz), jnp.float32),
        ],
        name="chebyshev",
    )


def rotate_kernel(n_all, n_x, nz):
    half, block = n_all // 2, n_all // n_x

    def body(mine, other, rows, out):
        core, x = chip_place(n_x)
        first = lax.div(lax.axis_index("band"), lax.axis_size("band") // n_x) + x
        near = rows[pl.ds(pl.multiple_of(core * half, half), half), :]
        far = rows[pl.ds(pl.multiple_of((1 - core) * half, half), half), :]
        for r in range(n_x):
            sums = jnp.dot(mine[r], near, preferred_element_type=jnp.float32)
            sums = sums + jnp.dot(other[r], far, preferred_element_type=jnp.float32)
            at = pl.multiple_of(lax.rem(first + r, n_x) * block, block)
            out[pl.ds(at, block), :] = sums.astype(jnp.bfloat16)

    vmem = pl.BlockSpec(memory_space=pltpu.VMEM)
    return pl.pallas_call(
        body,
        out_shape=pltpu.VMEM((n_all, nz), jnp.bfloat16),
        in_specs=[vmem, vmem, vmem],
        out_specs=vmem,
        name="rotate",
    )


def chip_place(n_x):
    dom = lax.axis_index("dom")
    return lax.rem(dom, 2), lax.rem(lax.div(dom, 2), n_x)


def in_vmem(x):
    return pltpu.with_memory_space_constraint(x, pltpu.VMEM)


def on_device(orbitals, potential, ritz):
    n_dom = lax.axis_size("dom")
    n_band = lax.axis_size("band")
    n_mine, _, cx, cy, nz = orbitals.shape
    n_all = ritz.shape[0]
    n_own = n_mine // n_dom
    n_x = n_dom // 4
    n_y = n_band // n_x
    core, _ = chip_place(n_x)

    pot = potential[0]
    high = lax.reduce_precision(pot, 8, 7)
    parts = jnp.stack([high, pot - high]).astype(jnp.bfloat16)
    parts = jnp.broadcast_to(parts[None], (n_dom, 2, cx, cy, nz))
    blocks = orbitals.reshape(n_dom, n_own, cx, cy, nz)
    blocks = jnp.concatenate([blocks, parts], axis=1)
    blocks = lax.all_to_all(blocks, "dom", 0, 0, tiled=True)
    kept, away = filter_kernel(n_dom, n_own, cx, cy, nz)(in_vmem(blocks))

    half = n_all // 2

    def split(d):
        return d // (2 * n_x), d // 2 % n_x, d % 2

    def from_x(value, step):
        pairs = []
        for d in range(n_dom):
            z, x, c = split(d)
            pairs.append((z * 2 * n_x + (x + step) % n_x * 2 + c, d))
        return lax.ppermute(value, "dom", pairs)

    turned = []
    for d in range(n_dom):
        z, x, c = split(d)
        for p in range(n_band):
            high_z, y = p // n_y, p % n_y
            near_z = 1 - z if x == 2 else z
            source = (near_z * 2 * n_x + x * 2 + c) * n_band + (high_z + x) % n_x * n_y + y
            turned.append((source, d * n_band + p))

    own = lax.dynamic_slice_in_dim(ritz.T, core * half, half, 1)
    own = lax.ppermute(own, ("dom", "band"), turned)
    many = jnp.broadcast_to(own[None], (n_y,) + own.shape)
    lines = [[z * n_y + y for y in range(n_y)] for z in range(n_x)]
    own = lax.all_to_all(many, "band", 0, 0, tiled=True, axis_index_groups=lines)
    own = own.reshape(n_y * n_mine, half)
    after = from_x(own, 1)
    before = from_x(own, -1)
    far = from_x(own, 2)
    mine = jnp.stack([own, after, far, before])
    other = lax.ppermute(mine, "dom", [(d, d ^ 1) for d in range(n_dom)])

    swapped = [(d, d ^ 1) for d in range(n_dom)]
    away = lax.ppermute(away, "dom", swapped)
    n_pair = n_dom // 2
    kept = kept.reshape(n_band * n_pair, n_own, nz)
    away = away.reshape(n_band * n_pair, n_own, nz)
    rows = jnp.where(
        core == 0, jnp.concatenate([kept, away], axis=1), jnp.concatenate([away, kept], axis=1)
    )
    group = [[b * n_dom + 2 * p + c for b in range(n_band) for p in range(n_pair)] for c in (0, 1)]
    rows = lax.all_to_all(
        rows, ("band", "dom"), 0, 0, tiled=True, axis_index_groups=group
    ).reshape(n_all, nz)

    rotated = rotate_kernel(n_all, n_x, nz)(in_vmem(mine), in_vmem(other), in_vmem(rows))
    rotated = lax.all_to_all(rotated.reshape(n_band, n_mine, nz), "band", 0, 0, tiled=True)
    rotated = rotated.transpose(1, 0, 2).astype(jnp.float32)
    return rotated.reshape(orbitals.shape)


def solution(mesh):
    in_specs = (P("band", "dom", None, None, None), P("dom", None, None, None), P(None, "band"))
    out_specs = P("band", "dom", None, None, None)
    return jax.shard_map(
        on_device, mesh=mesh, in_specs=in_specs, out_specs=out_specs, check_vma=False
    )
```

```python
import math

import jax
import jax.numpy as jnp
from jax import lax
from jax.experimental import pallas as pl
from jax.experimental.pallas import tpu as pltpu
from jax.sharding import PartitionSpec as P


DEG = 4

lower_bound = -1.5
cut_off = 1.0
upper_bound = 9.5
coef_zero = -2.5
coef_one = 4.0 / 3.0
coef_two = -1.0 / 12.0

PAD = 8


def filter_weights(degree):
    half_width = (upper_bound - cut_off) / 2.0
    centre = (upper_bound + cut_off) / 2.0
    sigma_now = half_width / (lower_bound - centre)
    first_scale = sigma_now / half_width
    inverse_gain = 2.0 / sigma_now
    weights = []
    for _ in range(1, degree):
        sigma_next = 1.0 / (inverse_gain - sigma_now)
        weights.append((2.0 * sigma_next / half_width, sigma_now * sigma_next))
        sigma_now = sigma_next
    return (centre, first_scale, weights)


def filter_kernel(n_dom, n_own, cx, cy, nz):
    side = math.isqrt(n_dom)
    gx, gy = side * cx, side * cy
    centre, first_scale, weights = filter_weights(DEG)
    row_stride = n_dom * n_own
    far_near = coef_two / coef_one

    def body(blocks, out, first, second, diag, ordered):
        for x in range(gx):
            for j in range(side):
                dom, inner = x // cx * side + j, x % cx
                for band in range(n_own):
                    value = blocks[dom, band, inner].astype(jnp.float32)
                    first[band, x, PAD + j * cy : PAD + (j + 1) * cy, :] = value
                    if j == 0:
                        first[band, x, PAD + gy : PAD + gy + PAD, :] = value[:PAD]
                    if j == side - 1:
                        first[band, x, 0:PAD, :] = value[cy - PAD :]
                pot = blocks[dom, n_own, inner].astype(jnp.float32) + blocks[
                    dom, n_own + 1, inner
                ].astype(jnp.float32)
                diag[x, j * cy : (j + 1) * cy, :] = pot + (-1.5 * coef_zero - centre)

        def sweep(cur, store):
            def one(band, carry):
                for y in range(0, gy, 8):

                    def rows(x, step):
                        return cur[band, x, PAD + y + step : PAD + y + step + 8, :]

                    mids = [rows(x, 0) for x in range(gx)]
                    sums = {}

                    def planes(x, step):
                        pair = tuple(sorted(((x - step) % gx, (x + step) % gx)))
                        if pair not in sums:
                            sums[pair] = mids[pair[0]] + mids[pair[1]]
                        return sums[pair]

                    for x in range(gx):
                        mid = mids[x]

                        def around(step):
                            lanes = pltpu.roll(mid, step, 1) + pltpu.roll(mid, nz - step, 1)
                            return planes(x, step) + (rows(x, -step) + rows(x, step)) + lanes

                        value = around(1) + far_near * around(2)
                        value = diag[x, y : y + 8, :] * mid + (-0.5 * coef_one) * value
                        store(band, x, y, value)
                return carry

            lax.fori_loop(0, n_own, one, 0)

        def put(ref, band, x, y, value):
            ref[band, x, PAD + y : PAD + y + 8, :] = value
            if y == 0:
                ref[band, x, PAD + gy : PAD + gy + PAD, :] = value
            if y == gy - 8:
                ref[band, x, 0:PAD, :] = value

        def start(band, x, y, value):
            put(second, band, x, y, value * first_scale)

        sweep(first, start)
        previous, current = first, second
        for scale_h, scale_x in weights[:-1]:

            def middle(band, x, y, value, previous=previous, scale_h=scale_h, scale_x=scale_x):
                before = previous[band, x, PAD + y : PAD + y + 8, :]
                put(previous, band, x, y, value * scale_h - scale_x * before)

            sweep(current, middle)
            previous, current = current, previous
        scale_h, scale_x = weights[-1]

        def last(band, x, y, value):
            value = value * scale_h - scale_x * previous[band, x, PAD + y : PAD + y + 8, :]
            dom = x // cx * side + y // cy
            base = (x % cx * cy + y % cy) * row_stride + dom * n_own + band
            ordered[pl.ds(base, 8, stride=row_stride), :] = value

        sweep(current, last)
        block = 128

        def store(n, carry):
            at = pl.multiple_of(n * block, block)
            out[pl.ds(at, block), :] = ordered[pl.ds(at, block), :].astype(jnp.bfloat16)
            return carry

        lax.fori_loop(0, out.shape[0] // block, store, 0)

    padded = pltpu.VMEM((n_own, gx, gy + 2 * PAD, nz), jnp.float32)
    rows_out = cx * cy * n_dom * n_own
    return pl.pallas_call(
        body,
        out_shape=pltpu.VMEM((rows_out, nz), jnp.bfloat16),
        in_specs=[pl.BlockSpec(memory_space=pltpu.VMEM)],
        out_specs=pl.BlockSpec(memory_space=pltpu.VMEM),
        scratch_shapes=[
            padded,
            padded,
            pltpu.VMEM((gx, gy, nz), jnp.float32),
            pltpu.VMEM((rows_out, nz), jnp.float32),
        ],
        name="chebyshev",
    )


def rotate_kernel(n_all, n_x, nz):
    half, block = n_all // 2, n_all // n_x

    def body(mine, other, rows, out):
        core, x = chip_place(n_x)
        z_lo = lax.div(lax.axis_index("dom"), 2 * n_x)
        z_hi = lax.div(lax.axis_index("band"), lax.axis_size("band") // n_x)
        first = z_hi + x + 2 * z_lo
        near = rows[pl.ds(pl.multiple_of(core * half, half), half), :]
        far = rows[pl.ds(pl.multiple_of((1 - core) * half, half), half), :]
        for r in range(n_x):
            sums = jnp.dot(mine[r], near, preferred_element_type=jnp.float32)
            sums = sums + jnp.dot(other[r], far, preferred_element_type=jnp.float32)
            at = pl.multiple_of(lax.rem(first + r, n_x) * block, block)
            out[pl.ds(at, block), :] = sums.astype(jnp.bfloat16)

    vmem = pl.BlockSpec(memory_space=pltpu.VMEM)
    return pl.pallas_call(
        body,
        out_shape=pltpu.VMEM((n_all, nz), jnp.bfloat16),
        in_specs=[vmem, vmem, vmem],
        out_specs=vmem,
        name="rotate",
    )


def chip_place(n_x):
    dom = lax.axis_index("dom")
    return lax.rem(dom, 2), lax.rem(lax.div(dom, 2), n_x)


def in_vmem(x):
    return pltpu.with_memory_space_constraint(x, pltpu.VMEM)


def on_device(orbitals, potential, ritz):
    n_dom = lax.axis_size("dom")
    n_band = lax.axis_size("band")
    n_mine, _, cx, cy, nz = orbitals.shape
    n_all = ritz.shape[0]
    n_own = n_mine // n_dom
    n_x = n_dom // 4
    n_y = n_band // n_x
    core, _ = chip_place(n_x)

    pot = potential[0]
    high = lax.reduce_precision(pot, 8, 7)
    parts = jnp.stack([high, pot - high]).astype(jnp.bfloat16)
    parts = jnp.broadcast_to(parts[None], (n_dom, 2, cx, cy, nz))
    blocks = orbitals.reshape(n_dom, n_own, cx, cy, nz)
    blocks = jnp.concatenate([blocks, parts], axis=1)
    blocks = lax.all_to_all(blocks, "dom", 0, 0, tiled=True)
    filtered = filter_kernel(n_dom, n_own, cx, cy, nz)(in_vmem(blocks))

    half = n_all // 2

    def split(d):
        return d // (2 * n_x), d // 2 % n_x, d % 2

    def from_x(value, step):
        pairs = []
        for d in range(n_dom):
            z, x, c = split(d)
            pairs.append((z * 2 * n_x + (x + step) % n_x * 2 + c, d))
        return lax.ppermute(value, "dom", pairs)

    turned = []
    for d in range(n_dom):
        z, x, c = split(d)
        for p in range(n_band):
            high_z, y = p // n_y, p % n_y
            near_z = 1 - z if x % 2 == 0 else z
            from_z = (high_z + x + 2 * z) % n_x
            source = (near_z * 2 * n_x + x * 2 + c) * n_band + from_z * n_y + y
            turned.append((source, d * n_band + p))

    own = lax.dynamic_slice_in_dim(ritz.T, core * half, half, 1)
    own = lax.ppermute(own, ("dom", "band"), turned)
    many = jnp.broadcast_to(own[None], (n_y,) + own.shape)
    lines = [[z * n_y + y for y in range(n_y)] for z in range(n_x)]
    own = lax.all_to_all(many, "band", 0, 0, tiled=True, axis_index_groups=lines)
    own = own.reshape(n_y * n_mine, half)
    after = from_x(own, 1)
    before = from_x(own, -1)
    partner = [(d, (d + n_dom // 2) % n_dom) for d in range(n_dom)]
    far = lax.ppermute(own, "dom", partner)
    mine = jnp.stack([own, after, far, before])
    other = lax.ppermute(mine, "dom", [(d, d ^ 1) for d in range(n_dom)])

    rows = lax.all_to_all(
        filtered.reshape(n_band * n_dom, n_own, nz), ("band", "dom"), 0, 0, tiled=True
    ).reshape(n_all, nz)

    rotated = rotate_kernel(n_all, n_x, nz)(in_vmem(mine), in_vmem(other), in_vmem(rows))
    rotated = lax.all_to_all(rotated.reshape(n_band, n_mine, nz), "band", 0, 0, tiled=True)
    rotated = rotated.transpose(1, 0, 2).astype(jnp.float32)
    return rotated.reshape(orbitals.shape)


def solution(mesh):
    in_specs = (P("band", "dom", None, None, None), P("dom", None, None, None), P(None, "band"))
    out_specs = P("band", "dom", None, None, None)
    return jax.shard_map(
        on_device, mesh=mesh, in_specs=in_specs, out_specs=out_specs, check_vma=False
    )
```

```python
import math

import jax
import jax.numpy as jnp
from jax import lax
from jax.experimental import pallas as pl
from jax.experimental.pallas import tpu as pltpu
from jax.sharding import PartitionSpec as P


DEG = 4

lower_bound = -1.5
cut_off = 1.0
upper_bound = 9.5
coef_zero = -2.5
coef_one = 4.0 / 3.0
coef_two = -1.0 / 12.0

PAD = 8


def filter_weights(degree):
    half_width = (upper_bound - cut_off) / 2.0
    centre = (upper_bound + cut_off) / 2.0
    sigma_now = half_width / (lower_bound - centre)
    first_scale = sigma_now / half_width
    inverse_gain = 2.0 / sigma_now
    weights = []
    for _ in range(1, degree):
        sigma_next = 1.0 / (inverse_gain - sigma_now)
        weights.append((2.0 * sigma_next / half_width, sigma_now * sigma_next))
        sigma_now = sigma_next
    return (centre, first_scale, weights)


def filter_kernel(n_dom, n_own, cx, cy, nz):
    side = math.isqrt(n_dom)
    gx, gy = side * cx, side * cy
    centre, first_scale, weights = filter_weights(DEG)
    row_stride = n_dom // 2 * n_own
    rows_out = cx * cy * row_stride
    far_near = coef_two / coef_one

    def body(blocks, out, away, first, second, diag, ordered):
        core, _ = chip_place(side)
        starts = [lax.bitwise_xor(core, c) * rows_out for c in (0, 1)]

        for x in range(gx):
            for j in range(side):
                dom, inner = x // cx * side + j, x % cx
                for band in range(n_own):
                    value = blocks[dom, band, inner].astype(jnp.float32)
                    first[band, x, PAD + j * cy : PAD + (j + 1) * cy, :] = value
                    if j == 0:
                        first[band, x, PAD + gy : PAD + gy + PAD, :] = value[:PAD]
                    if j == side - 1:
                        first[band, x, 0:PAD, :] = value[cy - PAD :]
                pot = blocks[dom, n_own, inner].astype(jnp.float32) + blocks[
                    dom, n_own + 1, inner
                ].astype(jnp.float32)
                diag[x, j * cy : (j + 1) * cy, :] = pot + (-1.5 * coef_zero - centre)

        def sweep(cur, store):
            def one(band, carry):
                for y in range(0, gy, 8):

                    def rows(x, step):
                        return cur[band, x, PAD + y + step : PAD + y + step + 8, :]

                    mids = [rows(x, 0) for x in range(gx)]
                    sums = {}

                    def planes(x, step):
                        pair = tuple(sorted(((x - step) % gx, (x + step) % gx)))
                        if pair not in sums:
                            sums[pair] = mids[pair[0]] + mids[pair[1]]
                        return sums[pair]

                    for x in range(gx):
                        mid = mids[x]

                        def around(step):
                            lanes = pltpu.roll(mid, step, 1) + pltpu.roll(mid, nz - step, 1)
                            return planes(x, step) + (rows(x, -step) + rows(x, step)) + lanes

                        value = around(1) + far_near * around(2)
                        value = diag[x, y : y + 8, :] * mid + (-0.5 * coef_one) * value
                        store(band, x, y, value)
                return carry

            lax.fori_loop(0, n_own, one, 0)

        def put(ref, band, x, y, value):
            ref[band, x, PAD + y : PAD + y + 8, :] = value
            if y == 0:
                ref[band, x, PAD + gy : PAD + gy + PAD, :] = value
            if y == gy - 8:
                ref[band, x, 0:PAD, :] = value

        def start(band, x, y, value):
            put(second, band, x, y, value * first_scale)

        sweep(first, start)
        previous, current = first, second
        for scale_h, scale_x in weights[:-1]:

            def middle(band, x, y, value, previous=previous, scale_h=scale_h, scale_x=scale_x):
                before = previous[band, x, PAD + y : PAD + y + 8, :]
                put(previous, band, x, y, value * scale_h - scale_x * before)

            sweep(current, middle)
            previous, current = current, previous
        scale_h, scale_x = weights[-1]

        def last(band, x, y, value):
            value = value * scale_h - scale_x * previous[band, x, PAD + y : PAD + y + 8, :]
            pair = (x // cx * side + y // cy) // 2
            base = (x % cx * cy + y % cy) * row_stride + pair * n_own + band
            base = base + starts[y // cy % 2]
            ordered[pl.ds(base, 8, stride=row_stride), :] = value

        sweep(current, last)
        block = 128

        def store(n, carry):
            at = pl.multiple_of(n * block, block)
            out[pl.ds(at, block), :] = ordered[pl.ds(at, block), :].astype(jnp.bfloat16)
            far = ordered[pl.ds(rows_out + at, block), :]
            away[pl.ds(at, block), :] = far.astype(jnp.bfloat16)
            return carry

        lax.fori_loop(0, out.shape[0] // block, store, 0)

    padded = pltpu.VMEM((n_own, gx, gy + 2 * PAD, nz), jnp.float32)
    vmem = pl.BlockSpec(memory_space=pltpu.VMEM)
    return pl.pallas_call(
        body,
        out_shape=[pltpu.VMEM((rows_out, nz), jnp.bfloat16)] * 2,
        in_specs=[vmem],
        out_specs=[vmem, vmem],
        scratch_shapes=[
            padded,
            padded,
            pltpu.VMEM((gx, gy, nz), jnp.float32),
            pltpu.VMEM((2 * rows_out, nz), jnp.float32),
        ],
        name="chebyshev",
    )


def rotate_kernel(n_all, n_x, nz):
    half, block = n_all // 2, n_all // n_x

    def body(mine, other, rows, out):
        core, x = chip_place(n_x)
        z_lo = lax.div(lax.axis_index("dom"), 2 * n_x)
        z_hi = lax.div(lax.axis_index("band"), lax.axis_size("band") // n_x)
        first = z_hi + x + 2 * z_lo
        near = rows[pl.ds(pl.multiple_of(core * half, half), half), :]
        far = rows[pl.ds(pl.multiple_of((1 - core) * half, half), half), :]
        for r in range(n_x):
            sums = jnp.dot(mine[r], near, preferred_element_type=jnp.float32)
            sums = sums + jnp.dot(other[r], far, preferred_element_type=jnp.float32)
            at = pl.multiple_of(lax.rem(first + r, n_x) * block, block)
            out[pl.ds(at, block), :] = sums.astype(jnp.bfloat16)

    vmem = pl.BlockSpec(memory_space=pltpu.VMEM)
    return pl.pallas_call(
        body,
        out_shape=pltpu.VMEM((n_all, nz), jnp.bfloat16),
        in_specs=[vmem, vmem, vmem],
        out_specs=vmem,
        name="rotate",
    )


def chip_place(n_x):
    dom = lax.axis_index("dom")
    return lax.rem(dom, 2), lax.rem(lax.div(dom, 2), n_x)


def in_vmem(x):
    return pltpu.with_memory_space_constraint(x, pltpu.VMEM)


def on_device(orbitals, potential, ritz):
    n_dom = lax.axis_size("dom")
    n_band = lax.axis_size("band")
    n_mine, _, cx, cy, nz = orbitals.shape
    n_all = ritz.shape[0]
    n_own = n_mine // n_dom
    n_x = n_dom // 4
    n_y = n_band // n_x
    core, _ = chip_place(n_x)

    pot = potential[0]
    high = lax.reduce_precision(pot, 8, 7)
    parts = jnp.stack([high, pot - high]).astype(jnp.bfloat16)
    parts = jnp.broadcast_to(parts[None], (n_dom, 2, cx, cy, nz))
    blocks = orbitals.reshape(n_dom, n_own, cx, cy, nz)
    blocks = jnp.concatenate([blocks, parts], axis=1)
    blocks = lax.all_to_all(blocks, "dom", 0, 0, tiled=True)
    kept, away = filter_kernel(n_dom, n_own, cx, cy, nz)(in_vmem(blocks))

    half = n_all // 2

    def split(d):
        return d // (2 * n_x), d // 2 % n_x, d % 2

    def from_x(value, step):
        pairs = []
        for d in range(n_dom):
            z, x, c = split(d)
            pairs.append((z * 2 * n_x + (x + step) % n_x * 2 + c, d))
        return lax.ppermute(value, "dom", pairs)

    turned = []
    for d in range(n_dom):
        z, x, c = split(d)
        for p in range(n_band):
            high_z, y = p // n_y, p % n_y
            near_z = 1 - z if x % 2 == 0 else z
            from_z = (high_z + x + 2 * z) % n_x
            source = (near_z * 2 * n_x + x * 2 + c) * n_band + from_z * n_y + y
            turned.append((source, d * n_band + p))

    own = lax.dynamic_slice_in_dim(ritz.T, core * half, half, 1)
    own = lax.ppermute(own, ("dom", "band"), turned)
    many = jnp.broadcast_to(own[None], (n_y,) + own.shape)
    lines = [[z * n_y + y for y in range(n_y)] for z in range(n_x)]
    own = lax.all_to_all(many, "band", 0, 0, tiled=True, axis_index_groups=lines)
    own = own.reshape(n_y * n_mine, half)
    after = from_x(own, 1)
    before = from_x(own, -1)
    partner = [(d, (d + n_dom // 2) % n_dom) for d in range(n_dom)]
    far = lax.ppermute(own, "dom", partner)
    mine = jnp.stack([own, after, far, before])
    other = lax.ppermute(mine, "dom", [(d, d ^ 1) for d in range(n_dom)])

    swapped = [(d, d ^ 1) for d in range(n_dom)]
    away = lax.ppermute(away, "dom", swapped)
    n_pair = n_dom // 2
    kept = kept.reshape(n_band * n_pair, n_own, nz)
    away = away.reshape(n_band * n_pair, n_own, nz)
    rows = lax.select(
        jnp.broadcast_to(core == 0, (n_band * n_pair, 2 * n_own, nz)),
        jnp.concatenate([kept, away], axis=1),
        jnp.concatenate([away, kept], axis=1),
    )
    group = [[b * n_dom + 2 * p + c for b in range(n_band) for p in range(n_pair)] for c in (0, 1)]
    rows = lax.all_to_all(
        rows, ("band", "dom"), 0, 0, tiled=True, axis_index_groups=group
    ).reshape(n_all, nz)

    rotated = rotate_kernel(n_all, n_x, nz)(in_vmem(mine), in_vmem(other), in_vmem(rows))
    rotated = lax.all_to_all(rotated.reshape(n_band, n_mine, nz), "band", 0, 0, tiled=True)
    rotated = rotated.transpose(1, 0, 2).astype(jnp.float32)
    return rotated.reshape(orbitals.shape)


def solution(mesh):
    in_specs = (P("band", "dom", None, None, None), P("dom", None, None, None), P(None, "band"))
    out_specs = P("band", "dom", None, None, None)
    return jax.shard_map(
        on_device, mesh=mesh, in_specs=in_specs, out_specs=out_specs, check_vma=False
    )
```

```python
import math

import jax
import jax.numpy as jnp
from jax import lax
from jax.experimental import pallas as pl
from jax.experimental.pallas import tpu as pltpu
from jax.sharding import PartitionSpec as P


DEG = 4

lower_bound = -1.5
cut_off = 1.0
upper_bound = 9.5
coef_zero = -2.5
coef_one = 4.0 / 3.0
coef_two = -1.0 / 12.0

PAD = 8


def filter_weights(degree):
    half_width = (upper_bound - cut_off) / 2.0
    centre = (upper_bound + cut_off) / 2.0
    sigma_now = half_width / (lower_bound - centre)
    first_scale = sigma_now / half_width
    inverse_gain = 2.0 / sigma_now
    weights = []
    for _ in range(1, degree):
        sigma_next = 1.0 / (inverse_gain - sigma_now)
        weights.append((2.0 * sigma_next / half_width, sigma_now * sigma_next))
        sigma_now = sigma_next
    return (centre, first_scale, weights)


def filter_kernel(n_dom, n_own, cx, cy, nz):
    side = math.isqrt(n_dom)
    gx, gy = side * cx, side * cy
    centre, first_scale, weights = filter_weights(DEG)
    row_stride = n_dom // 2 * n_own
    rows_out = cx * cy * row_stride
    far_near = coef_two / coef_one

    def body(blocks, out, away, first, second, diag, ordered):
        core, _ = chip_place(side)
        starts = [lax.bitwise_xor(core, c) * rows_out for c in (0, 1)]

        for x in range(gx):
            for j in range(side):
                dom, inner = x // cx * side + j, x % cx
                for band in range(n_own):
                    value = blocks[dom, band, inner].astype(jnp.float32)
                    first[band, x, PAD + j * cy : PAD + (j + 1) * cy, :] = value
                    if j == 0:
                        first[band, x, PAD + gy : PAD + gy + PAD, :] = value[:PAD]
                    if j == side - 1:
                        first[band, x, 0:PAD, :] = value[cy - PAD :]
                pot = blocks[dom, n_own, inner].astype(jnp.float32) + blocks[
                    dom, n_own + 1, inner
                ].astype(jnp.float32)
                diag[x, j * cy : (j + 1) * cy, :] = pot + (-1.5 * coef_zero - centre)

        def sweep(cur, store):
            def one(band, carry):
                for y in range(0, gy, 8):

                    def rows(x, step):
                        return cur[band, x, PAD + y + step : PAD + y + step + 8, :]

                    mids = [rows(x, 0) for x in range(gx)]
                    sums = {}

                    def planes(x, step):
                        pair = tuple(sorted(((x - step) % gx, (x + step) % gx)))
                        if pair not in sums:
                            sums[pair] = mids[pair[0]] + mids[pair[1]]
                        return sums[pair]

                    for x in range(gx):
                        mid = mids[x]

                        def around(step):
                            lanes = pltpu.roll(mid, step, 1) + pltpu.roll(mid, nz - step, 1)
                            return planes(x, step) + (rows(x, -step) + rows(x, step)) + lanes

                        value = around(1) + far_near * around(2)
                        value = diag[x, y : y + 8, :] * mid + (-0.5 * coef_one) * value
                        store(band, x, y, value)
                return carry

            lax.fori_loop(0, n_own, one, 0)

        def put(ref, band, x, y, value):
            ref[band, x, PAD + y : PAD + y + 8, :] = value
            if y == 0:
                ref[band, x, PAD + gy : PAD + gy + PAD, :] = value
            if y == gy - 8:
                ref[band, x, 0:PAD, :] = value

        def start(band, x, y, value):
            put(second, band, x, y, value * first_scale)

        sweep(first, start)
        previous, current = first, second
        for scale_h, scale_x in weights[:-1]:

            def middle(band, x, y, value, previous=previous, scale_h=scale_h, scale_x=scale_x):
                before = previous[band, x, PAD + y : PAD + y + 8, :]
                put(previous, band, x, y, value * scale_h - scale_x * before)

            sweep(current, middle)
            previous, current = current, previous
        scale_h, scale_x = weights[-1]

        def last(band, x, y, value):
            value = value * scale_h - scale_x * previous[band, x, PAD + y : PAD + y + 8, :]
            pair = (x // cx * side + y // cy) // 2
            base = (x % cx * cy + y % cy) * row_stride + pair * n_own + band
            base = base + starts[y // cy % 2]
            ordered[pl.ds(base, 8, stride=row_stride), :] = value

        sweep(current, last)
        block = 128

        def store(n, carry):
            at = pl.multiple_of(n * block, block)
            out[pl.ds(at, block), :] = ordered[pl.ds(at, block), :].astype(jnp.bfloat16)
            far = ordered[pl.ds(rows_out + at, block), :]
            away[pl.ds(at, block), :] = far.astype(jnp.bfloat16)
            return carry

        lax.fori_loop(0, out.shape[0] // block, store, 0)

    padded = pltpu.VMEM((n_own, gx, gy + 2 * PAD, nz), jnp.float32)
    vmem = pl.BlockSpec(memory_space=pltpu.VMEM)
    return pl.pallas_call(
        body,
        out_shape=[pltpu.VMEM((rows_out, nz), jnp.bfloat16)] * 2,
        in_specs=[vmem],
        out_specs=[vmem, vmem],
        scratch_shapes=[
            padded,
            padded,
            pltpu.VMEM((gx, gy, nz), jnp.float32),
            pltpu.VMEM((2 * rows_out, nz), jnp.float32),
        ],
        name="chebyshev",
    )


def pack_kernel(n_dom, n_own, cx, cy, nz):
    def body(bands, pot, out, parts, sems):
        copies = [pltpu.make_async_copy(bands, out.at[:, 0:n_own], sems.at[n_dom])]
        copies[0].start()
        value = pot[...]
        high = value.astype(jnp.bfloat16)
        parts[0] = high
        parts[1] = (value - high.astype(jnp.float32)).astype(jnp.bfloat16)
        for d in range(n_dom):
            copies.append(
                pltpu.make_async_copy(parts, out.at[d, n_own : n_own + 2], sems.at[d])
            )
            copies[-1].start()
        for copy in copies:
            copy.wait()

    return pl.pallas_call(
        body,
        out_shape=jax.ShapeDtypeStruct((n_dom, n_own + 2, cx, cy, nz), jnp.bfloat16),
        in_specs=[pl.BlockSpec(memory_space=pl.ANY), pl.BlockSpec(memory_space=pltpu.VMEM)],
        out_specs=pl.BlockSpec(memory_space=pl.ANY),
        scratch_shapes=[
            pltpu.VMEM((2, cx, cy, nz), jnp.bfloat16),
            pltpu.SemaphoreType.DMA((n_dom + 1,)),
        ],
        name="pack",
    )


def unpack_kernel(n_line, n_mine, nz):
    block = n_mine // 2

    def body(lines, out):
        first = pl.multiple_of(pl.program_id(0) * block, block)
        for line in range(n_line):
            value = lines[line, pl.ds(first, block), :].astype(jnp.float32)
            for at in range(0, block, 8):
                out[pl.ds(at * n_line + line, 8, stride=n_line), :] = value[at : at + 8]

    return pl.pallas_call(
        body,
        grid=(n_mine // block,),
        out_shape=jax.ShapeDtypeStruct((n_mine * n_line, nz), jnp.float32),
        in_specs=[pl.BlockSpec(memory_space=pltpu.VMEM)],
        out_specs=pl.BlockSpec((block * n_line, nz), lambda i: (i, 0)),
        name="unpack",
    )


def rotate_kernel(n_all, n_x, nz):
    half, block = n_all // 2, n_all // n_x

    def body(mine, other, rows, out):
        core, x = chip_place(n_x)
        z_lo = lax.div(lax.axis_index("dom"), 2 * n_x)
        z_hi = lax.div(lax.axis_index("band"), lax.axis_size("band") // n_x)
        first = z_hi + x + 2 * z_lo
        near = rows[pl.ds(pl.multiple_of(core * half, half), half), :]
        far = rows[pl.ds(pl.multiple_of((1 - core) * half, half), half), :]
        for r in range(n_x):
            sums = jnp.dot(mine[r], near, preferred_element_type=jnp.float32)
            sums = sums + jnp.dot(other[r], far, preferred_element_type=jnp.float32)
            at = pl.multiple_of(lax.rem(first + r, n_x) * block, block)
            out[pl.ds(at, block), :] = sums.astype(jnp.bfloat16)

    vmem = pl.BlockSpec(memory_space=pltpu.VMEM)
    return pl.pallas_call(
        body,
        out_shape=pltpu.VMEM((n_all, nz), jnp.bfloat16),
        in_specs=[vmem, vmem, vmem],
        out_specs=vmem,
        name="rotate",
    )


def chip_place(n_x):
    dom = lax.axis_index("dom")
    return lax.rem(dom, 2), lax.rem(lax.div(dom, 2), n_x)


def in_vmem(x):
    return pltpu.with_memory_space_constraint(x, pltpu.VMEM)


def on_device(orbitals, potential, ritz):
    n_dom = lax.axis_size("dom")
    n_band = lax.axis_size("band")
    n_mine, _, cx, cy, nz = orbitals.shape
    n_all = ritz.shape[0]
    n_own = n_mine // n_dom
    n_x = n_dom // 4
    n_y = n_band // n_x
    core, _ = chip_place(n_x)

    blocks = pack_kernel(n_dom, n_own, cx, cy, nz)(
        orbitals.reshape(n_dom, n_own, cx, cy, nz), potential[0]
    )
    blocks = lax.all_to_all(blocks, "dom", 0, 0, tiled=True)
    kept, away = filter_kernel(n_dom, n_own, cx, cy, nz)(in_vmem(blocks))

    half = n_all // 2

    def split(d):
        return d // (2 * n_x), d // 2 % n_x, d % 2

    def from_x(value, step):
        pairs = []
        for d in range(n_dom):
            z, x, c = split(d)
            pairs.append((z * 2 * n_x + (x + step) % n_x * 2 + c, d))
        return lax.ppermute(value, "dom", pairs)

    turned = []
    for d in range(n_dom):
        z, x, c = split(d)
        for p in range(n_band):
            high_z, y = p // n_y, p % n_y
            near_z = 1 - z if x % 2 == 0 else z
            from_z = (high_z + x + 2 * z) % n_x
            source = (near_z * 2 * n_x + x * 2 + c) * n_band + from_z * n_y + y
            turned.append((source, d * n_band + p))

    own = lax.dynamic_slice_in_dim(ritz.T, core * half, half, 1)
    own = lax.ppermute(own, ("dom", "band"), turned)
    many = jnp.broadcast_to(own[None], (n_y,) + own.shape)
    lines = [[z * n_y + y for y in range(n_y)] for z in range(n_x)]
    own = lax.all_to_all(many, "band", 0, 0, tiled=True, axis_index_groups=lines)
    own = own.reshape(n_y * n_mine, half)
    after = from_x(own, 1)
    before = from_x(own, -1)
    partner = [(d, (d + n_dom // 2) % n_dom) for d in range(n_dom)]
    far = lax.ppermute(own, "dom", partner)
    mine = jnp.stack([own, after, far, before])
    other = lax.ppermute(mine, "dom", [(d, d ^ 1) for d in range(n_dom)])

    swapped = [(d, d ^ 1) for d in range(n_dom)]
    away = lax.ppermute(away, "dom", swapped)
    n_pair = n_dom // 2
    kept = kept.reshape(n_band * n_pair, n_own, nz)
    away = away.reshape(n_band * n_pair, n_own, nz)
    lower = jnp.broadcast_to(core == 0, kept.shape)
    rows = jnp.stack([lax.select(lower, kept, away), lax.select(lower, away, kept)], axis=1)
    group = [[b * n_dom + 2 * p + c for b in range(n_band) for p in range(n_pair)] for c in (0, 1)]
    rows = lax.all_to_all(
        rows, ("band", "dom"), 0, 0, tiled=True, axis_index_groups=group
    ).reshape(n_all, nz)

    rotated = rotate_kernel(n_all, n_x, nz)(in_vmem(mine), in_vmem(other), in_vmem(rows))
    rotated = lax.all_to_all(rotated.reshape(n_band, n_mine, nz), "band", 0, 0, tiled=True)
    rotated = unpack_kernel(n_band, n_mine, nz)(in_vmem(rotated))
    return rotated.reshape(orbitals.shape)


def solution(mesh):
    in_specs = (P("band", "dom", None, None, None), P("dom", None, None, None), P(None, "band"))
    out_specs = P("band", "dom", None, None, None)
    return jax.shard_map(
        on_device, mesh=mesh, in_specs=in_specs, out_specs=out_specs, check_vma=False
    )
```

```python
import math

import jax
import jax.numpy as jnp
from jax import lax
from jax.experimental import pallas as pl
from jax.experimental.pallas import tpu as pltpu
from jax.sharding import PartitionSpec as P


DEG = 4

lower_bound = -1.5
cut_off = 1.0
upper_bound = 9.5
coef_zero = -2.5
coef_one = 4.0 / 3.0
coef_two = -1.0 / 12.0

PAD = 8


def filter_weights(degree):
    half_width = (upper_bound - cut_off) / 2.0
    centre = (upper_bound + cut_off) / 2.0
    sigma_now = half_width / (lower_bound - centre)
    first_scale = sigma_now / half_width
    inverse_gain = 2.0 / sigma_now
    weights = []
    for _ in range(1, degree):
        sigma_next = 1.0 / (inverse_gain - sigma_now)
        weights.append((2.0 * sigma_next / half_width, sigma_now * sigma_next))
        sigma_now = sigma_next
    return (centre, first_scale, weights)


def filter_kernel(n_dom, n_own, cx, cy, nz):
    side = math.isqrt(n_dom)
    gx, gy = side * cx, side * cy
    centre, first_scale, weights = filter_weights(DEG)
    row_stride = n_dom // 2 * n_own
    rows_out = cx * cy * row_stride
    far_near = coef_two / coef_one

    def body(blocks, out, away, first, second, diag, ordered):
        core, _ = chip_place(side)
        starts = [lax.bitwise_xor(core, c) * rows_out for c in (0, 1)]

        for x in range(gx):
            for j in range(side):
                dom, inner = x // cx * side + j, x % cx
                for band in range(n_own):
                    value = blocks[dom, band, inner].astype(jnp.float32)
                    first[band, x, PAD + j * cy : PAD + (j + 1) * cy, :] = value
                    if j == 0:
                        first[band, x, PAD + gy : PAD + gy + PAD, :] = value[:PAD]
                    if j == side - 1:
                        first[band, x, 0:PAD, :] = value[cy - PAD :]
                pot = blocks[dom, n_own, inner].astype(jnp.float32) + blocks[
                    dom, n_own + 1, inner
                ].astype(jnp.float32)
                diag[x, j * cy : (j + 1) * cy, :] = pot + (-1.5 * coef_zero - centre)

        def sweep(cur, store):
            def one(band, carry):
                for y in range(0, gy, 8):

                    def rows(x, step):
                        return cur[band, x, PAD + y + step : PAD + y + step + 8, :]

                    mids = [rows(x, 0) for x in range(gx)]
                    sums = {}

                    def planes(x, step):
                        pair = tuple(sorted(((x - step) % gx, (x + step) % gx)))
                        if pair not in sums:
                            sums[pair] = mids[pair[0]] + mids[pair[1]]
                        return sums[pair]

                    for x in range(gx):
                        mid = mids[x]

                        def around(step):
                            lanes = pltpu.roll(mid, step, 1) + pltpu.roll(mid, nz - step, 1)
                            return planes(x, step) + (rows(x, -step) + rows(x, step)) + lanes

                        value = around(1) + far_near * around(2)
                        value = diag[x, y : y + 8, :] * mid + (-0.5 * coef_one) * value
                        store(band, x, y, value)
                return carry

            lax.fori_loop(0, n_own, one, 0)

        def put(ref, band, x, y, value):
            ref[band, x, PAD + y : PAD + y + 8, :] = value
            if y == 0:
                ref[band, x, PAD + gy : PAD + gy + PAD, :] = value
            if y == gy - 8:
                ref[band, x, 0:PAD, :] = value

        def start(band, x, y, value):
            put(second, band, x, y, value * first_scale)

        sweep(first, start)
        previous, current = first, second
        for scale_h, scale_x in weights[:-1]:

            def middle(band, x, y, value, previous=previous, scale_h=scale_h, scale_x=scale_x):
                before = previous[band, x, PAD + y : PAD + y + 8, :]
                put(previous, band, x, y, value * scale_h - scale_x * before)

            sweep(current, middle)
            previous, current = current, previous
        scale_h, scale_x = weights[-1]

        def last(band, x, y, value):
            value = value * scale_h - scale_x * previous[band, x, PAD + y : PAD + y + 8, :]
            pair = (x // cx * side + y // cy) // 2
            base = (x % cx * cy + y % cy) * row_stride + pair * n_own + band
            base = base + starts[y // cy % 2]
            ordered[pl.ds(base, 8, stride=row_stride), :] = value

        sweep(current, last)
        block = 128

        def store(n, carry):
            at = pl.multiple_of(n * block, block)
            out[pl.ds(at, block), :] = ordered[pl.ds(at, block), :].astype(jnp.bfloat16)
            far = ordered[pl.ds(rows_out + at, block), :]
            away[pl.ds(at, block), :] = far.astype(jnp.bfloat16)
            return carry

        lax.fori_loop(0, out.shape[0] // block, store, 0)

    padded = pltpu.VMEM((n_own, gx, gy + 2 * PAD, nz), jnp.float32)
    vmem = pl.BlockSpec(memory_space=pltpu.VMEM)
    return pl.pallas_call(
        body,
        out_shape=[pltpu.VMEM((rows_out, nz), jnp.bfloat16)] * 2,
        in_specs=[vmem],
        out_specs=[vmem, vmem],
        scratch_shapes=[
            padded,
            padded,
            pltpu.VMEM((gx, gy, nz), jnp.float32),
            pltpu.VMEM((2 * rows_out, nz), jnp.float32),
        ],
        name="chebyshev",
    )


def pack_kernel(n_dom, n_own, cx, cy, nz):
    def body(bands, pot, out):
        value = pot[...]
        high = value.astype(jnp.bfloat16)
        low = (value - high.astype(jnp.float32)).astype(jnp.bfloat16)
        for d in range(n_dom):
            out[d, 0:n_own] = bands[d]
            out[d, n_own] = high
            out[d, n_own + 1] = low

    vmem = pl.BlockSpec(memory_space=pltpu.VMEM)
    return pl.pallas_call(
        body,
        out_shape=jax.ShapeDtypeStruct((n_dom, n_own + 2, cx, cy, nz), jnp.bfloat16),
        in_specs=[vmem, vmem],
        out_specs=vmem,
        name="pack",
    )


def rotate_kernel(n_all, n_x, nz):
    half, block = n_all // 2, n_all // n_x

    def body(mine, other, rows, out):
        core, x = chip_place(n_x)
        z_lo = lax.div(lax.axis_index("dom"), 2 * n_x)
        z_hi = lax.div(lax.axis_index("band"), lax.axis_size("band") // n_x)
        first = z_hi + x + 2 * z_lo
        near = rows[pl.ds(pl.multiple_of(core * half, half), half), :]
        far = rows[pl.ds(pl.multiple_of((1 - core) * half, half), half), :]
        for r in range(n_x):
            sums = jnp.dot(mine[r], near, preferred_element_type=jnp.float32)
            sums = sums + jnp.dot(other[r], far, preferred_element_type=jnp.float32)
            at = pl.multiple_of(lax.rem(first + r, n_x) * block, block)
            out[pl.ds(at, block), :] = sums.astype(jnp.bfloat16)

    vmem = pl.BlockSpec(memory_space=pltpu.VMEM)
    return pl.pallas_call(
        body,
        out_shape=pltpu.VMEM((n_all, nz), jnp.bfloat16),
        in_specs=[vmem, vmem, vmem],
        out_specs=vmem,
        name="rotate",
    )


def chip_place(n_x):
    dom = lax.axis_index("dom")
    return lax.rem(dom, 2), lax.rem(lax.div(dom, 2), n_x)


def in_vmem(x):
    return pltpu.with_memory_space_constraint(x, pltpu.VMEM)


def on_device(orbitals, potential, ritz):
    n_dom = lax.axis_size("dom")
    n_band = lax.axis_size("band")
    n_mine, _, cx, cy, nz = orbitals.shape
    n_all = ritz.shape[0]
    n_own = n_mine // n_dom
    n_x = n_dom // 4
    n_y = n_band // n_x
    core, _ = chip_place(n_x)

    blocks = pack_kernel(n_dom, n_own, cx, cy, nz)(
        orbitals.reshape(n_dom, n_own, cx, cy, nz), potential[0]
    )
    blocks = lax.all_to_all(blocks, "dom", 0, 0, tiled=True)
    kept, away = filter_kernel(n_dom, n_own, cx, cy, nz)(in_vmem(blocks))

    half = n_all // 2

    def split(d):
        return d // (2 * n_x), d // 2 % n_x, d % 2

    def from_x(value, step):
        pairs = []
        for d in range(n_dom):
            z, x, c = split(d)
            pairs.append((z * 2 * n_x + (x + step) % n_x * 2 + c, d))
        return lax.ppermute(value, "dom", pairs)

    turned = []
    for d in range(n_dom):
        z, x, c = split(d)
        for p in range(n_band):
            high_z, y = p // n_y, p % n_y
            near_z = 1 - z if x % 2 == 0 else z
            from_z = (high_z + x + 2 * z) % n_x
            source = (near_z * 2 * n_x + x * 2 + c) * n_band + from_z * n_y + y
            turned.append((source, d * n_band + p))

    own = lax.dynamic_slice_in_dim(ritz.T, core * half, half, 1)
    own = lax.ppermute(own, ("dom", "band"), turned)
    many = jnp.broadcast_to(own[None], (n_y,) + own.shape)
    lines = [[z * n_y + y for y in range(n_y)] for z in range(n_x)]
    own = lax.all_to_all(many, "band", 0, 0, tiled=True, axis_index_groups=lines)
    own = own.reshape(n_y * n_mine, half)
    after = from_x(own, 1)
    before = from_x(own, -1)
    partner = [(d, (d + n_dom // 2) % n_dom) for d in range(n_dom)]
    far = lax.ppermute(own, "dom", partner)
    mine = jnp.stack([own, after, far, before])
    other = lax.ppermute(mine, "dom", [(d, d ^ 1) for d in range(n_dom)])

    swapped = [(d, d ^ 1) for d in range(n_dom)]
    away = lax.ppermute(away, "dom", swapped)
    n_pair = n_dom // 2
    kept = kept.reshape(n_band * n_pair, n_own, nz)
    away = away.reshape(n_band * n_pair, n_own, nz)
    lower = jnp.broadcast_to(core == 0, kept.shape)
    rows = jnp.stack([lax.select(lower, kept, away), lax.select(lower, away, kept)], axis=1)
    group = [[b * n_dom + 2 * p + c for b in range(n_band) for p in range(n_pair)] for c in (0, 1)]
    rows = lax.all_to_all(
        rows, ("band", "dom"), 0, 0, tiled=True, axis_index_groups=group
    ).reshape(n_all, nz)

    rotated = rotate_kernel(n_all, n_x, nz)(in_vmem(mine), in_vmem(other), in_vmem(rows))
    rotated = lax.all_to_all(rotated.reshape(n_band, n_mine, nz), "band", 0, 0, tiled=True)
    rotated = rotated.transpose(1, 0, 2).astype(jnp.float32)
    return rotated.reshape(orbitals.shape)


def solution(mesh):
    in_specs = (P("band", "dom", None, None, None), P("dom", None, None, None), P(None, "band"))
    out_specs = P("band", "dom", None, None, None)
    return jax.shard_map(
        on_device, mesh=mesh, in_specs=in_specs, out_specs=out_specs, check_vma=False
    )
```

```python
import math

import jax
import jax.numpy as jnp
from jax import lax
from jax.experimental import pallas as pl
from jax.experimental.pallas import tpu as pltpu
from jax.sharding import PartitionSpec as P


DEG = 4

lower_bound = -1.5
cut_off = 1.0
upper_bound = 9.5
coef_zero = -2.5
coef_one = 4.0 / 3.0
coef_two = -1.0 / 12.0

PAD = 8


def filter_weights(degree):
    half_width = (upper_bound - cut_off) / 2.0
    centre = (upper_bound + cut_off) / 2.0
    sigma_now = half_width / (lower_bound - centre)
    first_scale = sigma_now / half_width
    inverse_gain = 2.0 / sigma_now
    weights = []
    for _ in range(1, degree):
        sigma_next = 1.0 / (inverse_gain - sigma_now)
        weights.append((2.0 * sigma_next / half_width, sigma_now * sigma_next))
        sigma_now = sigma_next
    return (centre, first_scale, weights)


def filter_kernel(n_dom, n_own, cx, cy, nz):
    side = math.isqrt(n_dom)
    gx, gy = side * cx, side * cy
    centre, first_scale, weights = filter_weights(DEG)
    row_stride = n_dom // 2 * n_own
    rows_out = cx * cy * row_stride
    far_near = coef_two / coef_one

    def body(blocks, out, away, first, second, diag, ordered):
        core, _ = chip_place(side)
        starts = [lax.bitwise_xor(core, c) * rows_out for c in (0, 1)]

        for x in range(gx):
            for j in range(side):
                dom, inner = x // cx * side + j, x % cx
                for band in range(n_own):
                    value = blocks[dom, band, inner].astype(jnp.float32)
                    first[band, x, PAD + j * cy : PAD + (j + 1) * cy, :] = value
                    if j == 0:
                        first[band, x, PAD + gy : PAD + gy + PAD, :] = value[:PAD]
                    if j == side - 1:
                        first[band, x, 0:PAD, :] = value[cy - PAD :]
                pot = blocks[dom, n_own, inner].astype(jnp.float32) + blocks[
                    dom, n_own + 1, inner
                ].astype(jnp.float32)
                diag[x, j * cy : (j + 1) * cy, :] = pot + (-1.5 * coef_zero - centre)

        def sweep(cur, store):
            def one(band, carry):
                for y in range(0, gy, 8):

                    def rows(x, step):
                        return cur[band, x, PAD + y + step : PAD + y + step + 8, :]

                    mids = [rows(x, 0) for x in range(gx)]
                    sums = {}

                    def planes(x, step):
                        pair = tuple(sorted(((x - step) % gx, (x + step) % gx)))
                        if pair not in sums:
                            sums[pair] = mids[pair[0]] + mids[pair[1]]
                        return sums[pair]

                    for x in range(gx):
                        mid = mids[x]

                        def around(step):
                            lanes = pltpu.roll(mid, step, 1) + pltpu.roll(mid, nz - step, 1)
                            return planes(x, step) + (rows(x, -step) + rows(x, step)) + lanes

                        value = around(1) + far_near * around(2)
                        value = diag[x, y : y + 8, :] * mid + (-0.5 * coef_one) * value
                        store(band, x, y, value)
                return carry

            lax.fori_loop(0, n_own, one, 0)

        def put(ref, band, x, y, value):
            ref[band, x, PAD + y : PAD + y + 8, :] = value
            if y == 0:
                ref[band, x, PAD + gy : PAD + gy + PAD, :] = value
            if y == gy - 8:
                ref[band, x, 0:PAD, :] = value

        def start(band, x, y, value):
            put(second, band, x, y, value * first_scale)

        sweep(first, start)
        previous, current = first, second
        for scale_h, scale_x in weights[:-1]:

            def middle(band, x, y, value, previous=previous, scale_h=scale_h, scale_x=scale_x):
                before = previous[band, x, PAD + y : PAD + y + 8, :]
                put(previous, band, x, y, value * scale_h - scale_x * before)

            sweep(current, middle)
            previous, current = current, previous
        scale_h, scale_x = weights[-1]

        def last(band, x, y, value):
            value = value * scale_h - scale_x * previous[band, x, PAD + y : PAD + y + 8, :]
            pair = (x // cx * side + y // cy) // 2
            base = (x % cx * cy + y % cy) * row_stride + pair * n_own + band
            base = base + starts[y // cy % 2]
            ordered[pl.ds(base, 8, stride=row_stride), :] = value

        sweep(current, last)
        block = 128

        def store(n, carry):
            at = pl.multiple_of(n * block, block)
            out[pl.ds(at, block), :] = ordered[pl.ds(at, block), :].astype(jnp.bfloat16)
            far = ordered[pl.ds(rows_out + at, block), :]
            away[pl.ds(at, block), :] = far.astype(jnp.bfloat16)
            return carry

        lax.fori_loop(0, out.shape[0] // block, store, 0)

    padded = pltpu.VMEM((n_own, gx, gy + 2 * PAD, nz), jnp.float32)
    vmem = pl.BlockSpec(memory_space=pltpu.VMEM)
    return pl.pallas_call(
        body,
        out_shape=[pltpu.VMEM((rows_out, nz), jnp.bfloat16)] * 2,
        in_specs=[vmem],
        out_specs=[vmem, vmem],
        scratch_shapes=[
            padded,
            padded,
            pltpu.VMEM((gx, gy, nz), jnp.float32),
            pltpu.VMEM((2 * rows_out, nz), jnp.float32),
        ],
        name="chebyshev",
    )


def rotate_kernel(n_all, n_x, nz):
    half, block = n_all // 2, n_all // n_x

    def body(mine, other, rows, out):
        core, x = chip_place(n_x)
        z_lo = lax.div(lax.axis_index("dom"), 2 * n_x)
        z_hi = lax.div(lax.axis_index("band"), lax.axis_size("band") // n_x)
        first = z_hi + x + 2 * z_lo
        step = 1 + (n_x - 2) * lax.rem(x, 2)
        near = rows[pl.ds(pl.multiple_of(core * half, half), half), :]
        far = rows[pl.ds(pl.multiple_of((1 - core) * half, half), half), :]
        for r in range(n_x):
            sums = jnp.dot(mine[r], near, preferred_element_type=jnp.float32)
            sums = sums + jnp.dot(other[r], far, preferred_element_type=jnp.float32)
            at = pl.multiple_of(lax.rem(first + r * step, n_x) * block, block)
            out[pl.ds(at, block), :] = sums.astype(jnp.bfloat16)

    vmem = pl.BlockSpec(memory_space=pltpu.VMEM)
    return pl.pallas_call(
        body,
        out_shape=pltpu.VMEM((n_all, nz), jnp.bfloat16),
        in_specs=[vmem, vmem, vmem],
        out_specs=vmem,
        name="rotate",
    )


def chip_place(n_x):
    dom = lax.axis_index("dom")
    return lax.rem(dom, 2), lax.rem(lax.div(dom, 2), n_x)


def in_vmem(x):
    return pltpu.with_memory_space_constraint(x, pltpu.VMEM)


def on_device(orbitals, potential, ritz):
    n_dom = lax.axis_size("dom")
    n_band = lax.axis_size("band")
    n_mine, _, cx, cy, nz = orbitals.shape
    n_all = ritz.shape[0]
    n_own = n_mine // n_dom
    n_x = n_dom // 4
    n_y = n_band // n_x
    core, _ = chip_place(n_x)

    pot = potential[0]
    high = lax.reduce_precision(pot, 8, 7)
    parts = jnp.stack([high, pot - high]).astype(jnp.bfloat16)
    parts = jnp.broadcast_to(parts[None], (n_dom, 2, cx, cy, nz))
    blocks = orbitals.reshape(n_dom, n_own, cx, cy, nz)
    blocks = jnp.concatenate([blocks, parts], axis=1)
    blocks = lax.all_to_all(blocks, "dom", 0, 0, tiled=True)
    kept, away = filter_kernel(n_dom, n_own, cx, cy, nz)(in_vmem(blocks))

    half = n_all // 2

    def split(d):
        return d // (2 * n_x), d // 2 % n_x, d % 2

    def beside_x(value, mask):
        pairs = []
        for d in range(n_dom):
            z, x, c = split(d)
            pairs.append((z * 2 * n_x + (x ^ mask) * 2 + c, d))
        return lax.ppermute(value, "dom", pairs)

    turned = []
    for d in range(n_dom):
        z, x, c = split(d)
        for p in range(n_band):
            high_z, y = p // n_y, p % n_y
            near_z = 1 - z if x % 2 == 0 else z
            from_z = (high_z + x + 2 * z) % n_x
            source = (near_z * 2 * n_x + x * 2 + c) * n_band + from_z * n_y + y
            turned.append((source, d * n_band + p))

    own = lax.dynamic_slice_in_dim(ritz.T, core * half, half, 1)
    own = lax.ppermute(own, ("dom", "band"), turned)
    many = jnp.broadcast_to(own[None], (n_y,) + own.shape)
    lines = [[z * n_y + y for y in range(n_y)] for z in range(n_x)]
    own = lax.all_to_all(many, "band", 0, 0, tiled=True, axis_index_groups=lines)
    own = own.reshape(n_y * n_mine, half)
    after = beside_x(own, 1)
    before = beside_x(own, n_x - 1)
    partner = [(d, (d + n_dom // 2) % n_dom) for d in range(n_dom)]
    far = lax.ppermute(own, "dom", partner)
    mine = jnp.stack([own, after, far, before])
    other = lax.ppermute(mine, "dom", [(d, d ^ 1) for d in range(n_dom)])

    swapped = [(d, d ^ 1) for d in range(n_dom)]
    away = lax.ppermute(away, "dom", swapped)
    n_pair = n_dom // 2
    kept = kept.reshape(n_band * n_pair, n_own, nz)
    away = away.reshape(n_band * n_pair, n_own, nz)
    rows = lax.select(
        jnp.broadcast_to(core == 0, (n_band * n_pair, 2 * n_own, nz)),
        jnp.concatenate([kept, away], axis=1),
        jnp.concatenate([away, kept], axis=1),
    )
    group = [[b * n_dom + 2 * p + c for b in range(n_band) for p in range(n_pair)] for c in (0, 1)]
    rows = lax.all_to_all(
        rows, ("band", "dom"), 0, 0, tiled=True, axis_index_groups=group
    ).reshape(n_all, nz)

    rotated = rotate_kernel(n_all, n_x, nz)(in_vmem(mine), in_vmem(other), in_vmem(rows))
    rotated = lax.all_to_all(rotated.reshape(n_band, n_mine, nz), "band", 0, 0, tiled=True)
    rotated = rotated.transpose(1, 0, 2).astype(jnp.float32)
    return rotated.reshape(orbitals.shape)


def solution(mesh):
    in_specs = (P("band", "dom", None, None, None), P("dom", None, None, None), P(None, "band"))
    out_specs = P("band", "dom", None, None, None)
    return jax.shard_map(
        on_device, mesh=mesh, in_specs=in_specs, out_specs=out_specs, check_vma=False
    )
```
